32 devices in a mesh: dom: 32 (over z, y, x, core).
Axes of the slice: x: 2, y: 2, z: 4, core: 2. Of those that a mesh axis runs over, the one named last changes fastest.
Arguments:
- states: float32 [16384, 128], P('dom'), may hold values from -6 to 6
- diag_blocks: float32 [128, 128, 128], P('dom'), may hold values from -0.5 to 0.5
- couplings: float32 [128, 128, 128], P('dom'), may hold values from -0.5 to 0.5
Outputs:
- orthonormal: float32 [16384, 128], P('dom')
- projected: float32 [128, 128], replicated
The draws below stay inside these ranges and needn't reach their ends.
All inputs are finite; a program needn't handle non-finite values.
Results may differ from the reference program's by a relative error of at most 0.00012.
Values sent between devices are 32-bit elements; how exact they have to be, the bound alone decides.
No kernel may reach another device: no remote copies, remote signals or barrier semaphores. Data moves between devices by JAX's collectives and lax.ppermute only.
A program may use at most 64 MiB of HBM per device.

```python
import math
import jax
import jax.numpy as jnp
from jax import lax

NB = 128
BLOCK = 128
NODES = 16384
BLOCKS = 128


def block_levels(own_key, dims, pieces, least, largest):
    def one(position, shards_of):
        steps = jax.random.uniform(jax.random.fold_in(jax.random.fold_in(own_key, 6), position), (shards_of,), jnp.float32, least / len(pieces), largest / len(pieces))
        return jnp.repeat(jnp.exp(steps), dims[position] // shards_of).reshape((-1,) + (1,) * (len(dims) - position - 1))

    gain = one(*pieces[0])
    for cut in pieces[1:]:
        gain = gain * one(*cut)
    return gain


def noise(key, shape, spread, reach, shards=(), kind=jnp.bfloat16):
    loudness = block_levels(key, shape, shards, -0.22, 0.18) if shards else 1.0
    values = jax.random.normal(key, shape, jnp.float32) * spread * loudness
    return jnp.minimum(jnp.maximum(values, -reach), reach).astype(kind)


def setup_inputs(seed: int = 0) -> dict:
    seeds = jax.random.split(jax.random.key(seed), 4)
    return {
        "states": noise(seeds[0], (NODES, NB), 1.0, 6.0, ((0, 32),), jnp.float32),
        "diag_blocks": noise(seeds[1], (BLOCKS, BLOCK, BLOCK), BLOCK ** -0.5, 0.5, ((0, 32),), jnp.float32),
        "couplings": noise(seeds[2], (BLOCKS, BLOCK, BLOCK), BLOCK ** -0.5, 0.5, ((0, 32),), jnp.float32),
    }


center = 0.5
half_width = 4.0

def lower_solve(factor, values):
    return lax.linalg.triangular_solve(factor, values, left_side=True, lower=True)

def apply_band(extended, diag_ext, coup_ext):
    inside = jnp.einsum('bij,bjs->bis', diag_ext[1:-1], extended[1:-1], precision=lax.Precision.HIGHEST)
    upward = jnp.einsum('bij,bjs->bis', coup_ext[1:-1], extended[2:], precision=lax.Precision.HIGHEST)
    downward = jnp.einsum('bji,bjs->bis', coup_ext[:-2], extended[:-2], precision=lax.Precision.HIGHEST)
    return inside + upward + downward

def pad_blocks(values):
    return jnp.pad(values, ((1, 1), (0, 0), (0, 0)))

def reference(states, diag_blocks, couplings):
    symmetric = 0.5 * (diag_blocks + jnp.swapaxes(diag_blocks, 1, 2))
    diag_ext = pad_blocks(symmetric)
    coup_ext = pad_blocks(couplings)
    field = states.reshape(BLOCKS, BLOCK, NB)
    first = (apply_band(pad_blocks(field), diag_ext, coup_ext) - center * field) / half_width
    filtered = 2.0 * (apply_band(pad_blocks(first), diag_ext, coup_ext) - center * first) / half_width - field
    image = apply_band(pad_blocks(filtered), diag_ext, coup_ext)
    flat = filtered.reshape(NODES, NB)
    correlation = jnp.einsum('ns,nt->st', flat, flat, precision=lax.Precision.HIGHEST)
    mixed = jnp.einsum('ns,nt->st', flat, image.reshape(NODES, NB), precision=lax.Precision.HIGHEST)
    lower = jnp.linalg.cholesky(correlation)
    orthonormal = lower_solve(lower, flat.T).T * math.sqrt(NODES)
    left = lower_solve(lower, mixed)
    projected = lower_solve(lower, left.T).T
    return (orthonormal, projected)
```

```python
import math

import jax
import jax.numpy as jnp
from jax import lax
from jax.experimental import pallas as pl
from jax.experimental.pallas import tpu as pltpu
from jax.sharding import PartitionSpec as P

center = 0.5
half_width = 4.0
exact = lax.Precision.HIGHEST
vmem = pl.BlockSpec(memory_space=pltpu.VMEM)
smem = pl.BlockSpec(memory_space=pltpu.SMEM)


def mm(a, b):
    return lax.dot_general(
        a, b, (((1,), (0,)), ((), ())), precision=exact, preferred_element_type=jnp.float32
    )


def mm_tn(a, b):
    return lax.dot_general(
        a, b, (((0,), (0,)), ((), ())), precision=exact, preferred_element_type=jnp.float32
    )


def mm_nt(a, b):
    return lax.dot_general(
        a, b, (((1,), (1,)), ((), ())), precision=exact, preferred_element_type=jnp.float32
    )


def iotas(shape):
    return (
        lax.broadcasted_iota(jnp.int32, shape, 0),
        lax.broadcasted_iota(jnp.int32, shape, 1),
    )


def prepare(where_ref, s_ref, d_ref, c_ref, even_ref, odd_ref, sym_ref, clast_ref, first_ref, pass_ref):
    nblocks, block, unused = d_ref.shape
    last = nblocks - 1
    rows, cols = iotas((block, block))
    shift = jnp.where(rows == cols, center, 0.0)
    s = [s_ref[b * block : (b + 1) * block, :] for b in range(nblocks)]
    c = [c_ref[b] for b in range(nblocks)]
    c[last] = jnp.where(where_ref[1] == 1, jnp.zeros_like(c[last]), c[last])
    clast_ref[...] = c[last]
    sym = []
    for b in range(nblocks):
        d = d_ref[b]
        sym.append(0.5 * (d + d.T) - shift)
        sym_ref[b] = sym[b]
    first = []
    for b in range(nblocks):
        acc = mm(sym[b], s[b])
        if b < last:
            acc += mm(c[b], s[b + 1])
        if b > 0:
            acc += mm_tn(c[b - 1], s[b - 1])
        first.append(acc / half_width)
        first_ref[b * block : (b + 1) * block, :] = first[b]
    onward = mm_tn(c[last], s[last])
    pass_ref[...] = onward
    second = 2.0 * (mm(sym[0], first[0]) + mm(c[0], first[1])) / half_width - s[0]
    again = mm_tn(c[last], first[last])

    def put(left_ref, right_ref):
        left_ref[0] = s[0]
        left_ref[1] = first[0]
        left_ref[2] = second
        left_ref[3] = sym[0]
        right_ref[0] = onward
        right_ref[1] = again
        right_ref[2] = c[last]
        right_ref[3] = jnp.zeros_like(s[0])

    @pl.when(where_ref[0] == 0)
    def _():
        put(odd_ref, even_ref)

    @pl.when(where_ref[0] != 0)
    def _():
        put(even_ref, odd_ref)


def project(where_ref, s_ref, c_ref, sym_ref, clast_ref, first_ref, pass_ref, even_ref, odd_ref, filt_ref, sums_ref):
    nblocks, block, unused = c_ref.shape
    last = nblocks - 1
    rows, cols = iotas((block, block))
    even_is_right = where_ref[0] == 0
    s = [s_ref[b * block : (b + 1) * block, :] for b in range(nblocks)]
    first = [first_ref[b * block : (b + 1) * block, :] for b in range(nblocks)]
    sym = [sym_ref[b] for b in range(nblocks)]
    c = [c_ref[b] for b in range(last)] + [clast_ref[...]]
    right = [jnp.where(even_is_right, even_ref[k], odd_ref[k]) for k in range(4)]
    left = [jnp.where(even_is_right, odd_ref[k], even_ref[k]) for k in range(3)]
    onward = pass_ref[...]
    scale = 2.0 / half_width
    behind = left[1] + mm_tn(left[2], mm(left[2], s[0])) / half_width
    ahead = right[1] + onward / half_width
    first[0] = first[0] + left[0] / half_width
    first[last] = first[last] + mm(c[last], right[0]) / half_width
    first.append(ahead)
    filtered = []
    for b in range(nblocks):
        acc = mm(sym[b], first[b]) + mm(c[b], first[b + 1])
        acc += behind if b == 0 else mm_tn(c[b - 1], first[b - 1])
        filtered.append(scale * acc - s[b])
        filt_ref[b * block : (b + 1) * block, :] = filtered[b]
    beyond = right[2] + scale * (mm(right[3], onward) / half_width + mm_tn(c[last], first[last]))
    filtered.append(beyond)
    correlation = mm_tn(filtered[0], filtered[0])
    half = None
    for b in range(nblocks):
        image = 0.5 * (mm(sym[b], filtered[b]) + center * filtered[b]) + mm(c[b], filtered[b + 1])
        if b:
            correlation += mm_tn(filtered[b], filtered[b])
        term = mm_tn(filtered[b], image)
        half = term if half is None else half + term
    mixed = half + half.T
    width = mixed.shape[0]
    rows, cols = iotas((width, width))
    sums_ref[0:width, :] = jnp.where(rows >= cols, correlation, mixed)
    diagonal = jnp.sum(jnp.where(rows == cols, mixed, 0.0), axis=0, keepdims=True)
    sums_ref[width : width + 8, :] = jnp.broadcast_to(diagonal, (8, width))


def finish(total_nodes, sums_ref, filt_ref, orth_ref, proj_ref, inv_ref):
    width = filt_ref.shape[1]
    tiles = width // 8
    packed = sums_ref[0:width, :]
    rows, cols = iotas((width, width))
    upper = jnp.where(rows < cols, packed, 0.0)
    diagonal = jnp.where(rows == cols, sums_ref[width : width + 1, :], 0.0)
    mixed = upper + upper.T + diagonal
    low = jnp.where(rows >= cols, packed, 0.0)
    full = low + jnp.where(rows > cols, packed, 0.0).T
    sub, lane = iotas((8, width))
    work = [full[8 * t : 8 * t + 8, :] for t in range(tiles)]
    for p in range(tiles):
        at = 8 * p
        inside = (lane >= at) & (lane < at + 8)
        row = [jnp.broadcast_to(work[p][j : j + 1, :], (8, width)) for j in range(8)]
        a = {}
        for i in range(8):
            for j in range(i + 1):
                a[i, j] = jnp.broadcast_to(row[i][:, at + j : at + j + 1], (8, width))
        m, recip = {}, []
        for j in range(8):
            recip.append(1.0 / a[j, j])
            for i in range(j + 1, 8):
                m[i, j] = a[i, j] * recip[j]
            for i in range(j + 1, 8):
                for k in range(j + 1, i + 1):
                    a[i, k] = a[i, k] - m[i, j] * a[k, j]
        pivot = []
        for j in range(8):
            r = jnp.where(inside, jnp.where(lane == at + j, 1.0, 0.0), row[j])
            for k in range(j):
                r = r - m[j, k] * pivot[k]
            pivot.append(r)
        out = jnp.zeros((8, width), jnp.float32)
        for j in range(8):
            out = jnp.where(sub == j, pivot[j] * lax.rsqrt(a[j, j]), out)
        inv_ref[at : at + 8, :] = jnp.where(lane <= sub + at, out, 0.0)
        for t in range(p + 1, tiles):
            w = []
            for j in range(8):
                x = jnp.broadcast_to(work[t][:, at + j : at + j + 1], (8, width))
                for k in range(j):
                    x = x - w[k] * m[j, k]
                w.append(x)
            acc = jnp.where(inside, 0.0, work[t])
            for j in range(8):
                acc = acc - (w[j] * recip[j]) * pivot[j]
            work[t] = acc
    inv = inv_ref[...]
    orth_ref[...] = mm_nt(filt_ref[...], inv) * math.sqrt(total_nodes)
    proj_ref[...] = mm_nt(mm(inv, mixed), inv)


def shape(*dims):
    return jax.ShapeDtypeStruct(dims, jnp.float32)


def total_over(values, axis):
    count = lax.axis_size(axis)
    index = lax.axis_index(axis)
    stride = 1
    while stride < count:
        left = count // stride
        radix = next(r for r in range(2, left + 1) if left % r == 0)
        if radix == 2:
            route = [(i, i + stride if (i // stride) % 2 == 0 else i - stride) for i in range(count)]
            values = values + lax.ppermute(values, axis, route)
        else:
            place = (index // stride) % radix
            parts = [values]
            for hop in range(1, radix):
                route = []
                for i in range(count):
                    digit = (i // stride) % radix
                    route.append((i, i + ((digit - hop) % radix - digit) * stride))
                parts.append(lax.ppermute(values, axis, route))
            stacked = jnp.stack(parts)
            total = None
            for digit in range(radix):
                term = lax.dynamic_index_in_dim(stacked, (digit - place) % radix, 0, keepdims=False)
                total = term if total is None else total + term
            values = total
        stride *= radix
    return values


def swap(values, axis, start):
    count = lax.axis_size(axis)
    route = []
    for i in range(start, count - 1, 2):
        route += [(i, i + 1), (i + 1, i)]
    return lax.ppermute(values, axis, route)


def body(states, diag_blocks, couplings):
    nodes_dev, width = states.shape
    nblocks, block, unused = diag_blocks.shape
    devices = lax.axis_size("dom")
    index = lax.axis_index("dom")
    where = jnp.stack([index % 2, (index == devices - 1).astype(jnp.int32)])
    params = pltpu.CompilerParams(vmem_limit_bytes=48 << 20)
    cross = shape(4, block, width)
    even, odd, sym, clast, first, onward = pl.pallas_call(
        prepare,
        out_shape=(cross, cross, shape(nblocks, block, block), shape(block, block), shape(nodes_dev, width), shape(block, width)),
        in_specs=[smem, vmem, vmem, vmem],
        out_specs=(vmem,) * 6,
        compiler_params=params,
        name="prepare",
    )(where, states, diag_blocks, couplings)
    even = swap(even, "dom", 0)
    odd = swap(odd, "dom", 1)
    filtered, sums = pl.pallas_call(
        project,
        out_shape=(shape(nodes_dev, width), shape(width + 8, width)),
        in_specs=[smem] + [vmem] * 8,
        out_specs=(vmem,) * 2,
        compiler_params=params,
        name="project",
    )(where, states, couplings, sym, clast, first, onward, even, odd)
    sums = total_over(sums, "dom")
    orthonormal, projected, unused = pl.pallas_call(
        lambda *refs: finish(nodes_dev * devices, *refs),
        out_shape=(shape(nodes_dev, width), shape(width, width), shape(width, width)),
        in_specs=[vmem] * 2,
        out_specs=(vmem,) * 3,
        compiler_params=params,
        name="finish",
    )(sums, filtered)
    return orthonormal, projected


def solution(mesh):
    in_specs = (P("dom", None), P("dom", None, None), P("dom", None, None))
    out_specs = (P("dom", None), P())
    return jax.shard_map(body, mesh=mesh, in_specs=in_specs, out_specs=out_specs, check_vma=False)
```

```python
import math

import jax
import jax.numpy as jnp
from jax import lax
from jax.experimental import pallas as pl
from jax.experimental.pallas import tpu as pltpu
from jax.sharding import PartitionSpec as P

center = 0.5
half_width = 4.0
scale = 2.0 / half_width
here = pl.BlockSpec(memory_space=pltpu.VMEM)
far = pl.BlockSpec(memory_space=pltpu.HBM)


def two(x):
    high = x.astype(jnp.bfloat16)
    return high, (x - high.astype(jnp.float32)).astype(jnp.bfloat16)


def three(x):
    high = x.astype(jnp.bfloat16)
    rest = x - high.astype(jnp.float32)
    mid = rest.astype(jnp.bfloat16)
    return high, mid, (rest - mid.astype(jnp.float32)).astype(jnp.bfloat16)


def dot(a, b, on=(1, 0)):
    return lax.dot_general(a, b, (((on[0],), (on[1],)), ((), ())), preferred_element_type=jnp.float32)


def left3(x, axis=1):
    high, low = two(x)
    return jnp.concatenate([high, high, low], axis)


def right3(x, axis=0):
    high, low = two(x)
    return jnp.concatenate([high, low, high], axis)


def left6(x, axis=1):
    high, mid, low = three(x)
    return jnp.concatenate([high, high, mid, high, low, mid], axis)


def right6(x, axis=0):
    high, mid, low = three(x)
    return jnp.concatenate([high, mid, high, low, high, mid], axis)


def iotas(shape):
    return (
        lax.broadcasted_iota(jnp.int32, shape, 0),
        lax.broadcasted_iota(jnp.int32, shape, 1),
    )


def symmetric(d):
    rows, cols = iotas(d.shape)
    return 0.5 * (d + d.T) - jnp.where(rows == cols, center, 0.0)


def leftward(s0, s1, s2, sym0, sym1, c0, c1, out_ref):
    l0, r0, r1 = left3(sym0), right3(s0), right3(s1)
    c0l = left3(c0)
    part = (dot(l0, r0) + dot(c0l, r1)) / half_width
    first1 = (dot(left3(sym1), r1) + dot(left3(c1), right3(s2)) + dot(left3(c0.T), r0)) / half_width
    out_ref[0] = s0
    out_ref[1] = part
    out_ref[2] = scale * (dot(l0, right3(part)) + dot(c0l, right3(first1))) - s0
    out_ref[3] = sym0


def rightward(s_prev, s_last, sym_last, c_prev, c_last, out_ref):
    rl = right3(s_last)
    part = (dot(left3(sym_last), rl) + dot(left3(c_prev.T), right3(s_prev))) / half_width
    turned = left3(c_last.T)
    out_ref[0] = dot(turned, rl)
    out_ref[1] = dot(turned, right3(part))
    out_ref[2] = c_last
    out_ref[3] = jnp.zeros_like(c_last)


def edge(axis, s_hbm, d_hbm, c_hbm, odd_ref, s_ref, d_ref, c_ref, sems):
    nblocks = d_hbm.shape[0]
    last = nblocks - 1
    parity = lax.rem(lax.axis_index(axis), 2)
    is_last = lax.axis_index(axis) == lax.axis_size(axis) - 1
    copies = []
    for k, (source, target) in enumerate(((s_hbm, s_ref), (d_hbm, d_ref), (c_hbm, c_ref))):
        copies.append(pltpu.make_async_copy(source, target, sems.at[k]))
    for copy in copies:
        copy.start()
    for copy in copies:
        copy.wait()

    @pl.when(is_last)
    def _():
        c_ref[last] = jnp.zeros_like(c_ref[last])

    @pl.when(parity == 0)
    def _():
        leftward(s_ref[0], s_ref[1], s_ref[2], symmetric(d_ref[0]), symmetric(d_ref[1]), c_ref[0], c_ref[1], odd_ref)

    @pl.when(parity != 0)
    def _():
        rightward(s_ref[last - 1], s_ref[last], symmetric(d_ref[last]), c_ref[last - 1], c_ref[last], odd_ref)


def inner(axis, s_ref, d_ref, c_ref, even_ref, sym_ref, cl_ref, ct_ref, first_ref, pre_ref, pass_ref):
    nblocks = d_ref.shape[0]
    last = nblocks - 1
    parity = lax.rem(lax.axis_index(axis), 2)

    @pl.when(parity != 0)
    def _():
        leftward(s_ref[0], s_ref[1], s_ref[2], symmetric(d_ref[0]), symmetric(d_ref[1]), c_ref[0], c_ref[1], even_ref)

    @pl.when(parity == 0)
    def _():
        rightward(s_ref[last - 1], s_ref[last], symmetric(d_ref[last]), c_ref[last - 1], c_ref[last], even_ref)

    s = [s_ref[b] for b in range(nblocks)]
    sr = [right3(x) for x in s]
    for b in range(nblocks):
        sym_ref[b] = left3(symmetric(d_ref[b]))
        cl_ref[b] = left3(c_ref[b])
        ct_ref[b] = left3(c_ref[b].T)
    first = []
    for b in range(nblocks):
        acc = dot(sym_ref[b], sr[b])
        if b < last:
            acc += dot(cl_ref[b], sr[b + 1])
        if b > 0:
            acc += dot(ct_ref[b - 1], sr[b - 1])
        first.append(acc / half_width)
        first_ref[b] = first[b]
    pass_ref[...] = dot(ct_ref[last], sr[last])
    fr = [right3(x) for x in first]
    for b in range(nblocks):
        acc = None
        terms = []
        if 0 < b < last:
            terms.append((sym_ref, b, b))
        if b + 1 < last:
            terms.append((cl_ref, b, b + 1))
        if b > 1:
            terms.append((ct_ref, b - 1, b - 1))
        for ref, which, operand in terms:
            term = dot(ref[which], fr[operand])
            acc = term if acc is None else acc + term
        pre_ref[b] = -s[b] if acc is None else scale * acc - s[b]


def project(axis, s_ref, sym_ref, cl_ref, ct_ref, first_ref, pre_ref, pass_ref, even_ref, odd_ref, filt_ref, keep_ref, send_ref):
    nblocks, block, unused = s_ref.shape
    last = nblocks - 1
    parity = lax.rem(lax.axis_index(axis), 2)
    right = [jnp.where(parity == 0, even_ref[k], odd_ref[k]) for k in range(4)]
    left = [jnp.where(parity == 0, odd_ref[k], even_ref[k]) for k in range(3)]
    onward = pass_ref[...]
    tail = first_ref[last] + dot(cl_ref[last], right3(right[0])) / half_width
    head = first_ref[0] + left[0] / half_width
    ahead = right[1] + onward / half_width
    back = dot(left3(left[2]), right3(s_ref[0]))
    behind = left[1] + dot(left3(left[2].T), right3(back)) / half_width
    tail_r, head_r = right3(tail), right3(head)
    filtered = [pre_ref[b] for b in range(nblocks)]
    filtered[0] += scale * (dot(sym_ref[0], head_r) + behind)
    filtered[1] += scale * dot(ct_ref[0], head_r)
    filtered[last - 1] += scale * dot(cl_ref[last - 1], tail_r)
    filtered[last] += scale * (dot(sym_ref[last], tail_r) + dot(cl_ref[last], right3(ahead)))
    beyond = right[2] + scale * (dot(left3(right[3]), right3(onward)) / half_width + dot(ct_ref[last], tail_r))
    filtered.append(beyond)
    fr = [right3(x) for x in filtered]
    both = []
    for b in range(nblocks):
        filt_ref[b] = filtered[b]
        image = 0.5 * (dot(sym_ref[b], fr[b]) + center * filtered[b]) + dot(cl_ref[b], fr[b + 1])
        both.append(jnp.concatenate([filtered[b], image], 1))
    total = None
    for b in range(nblocks):
        term = dot(left6(filtered[b], 0), right6(both[b], 0), (0, 0))
        total = term if total is None else total + term
    width = filtered[0].shape[1]
    correlation, half = total[:, :width], total[:, width:]
    mixed = half + half.T
    rows, cols = iotas((width, width))
    packed = jnp.where(rows >= cols, correlation, mixed)
    diagonal = jnp.sum(jnp.where(rows == cols, mixed, 0.0), axis=0, keepdims=True)
    mid = width // 2

    def put(top_ref, low_ref):
        top_ref[0:mid, :] = packed[:mid]
        top_ref[mid : mid + 8, :] = jnp.broadcast_to(diagonal, (8, width))
        low_ref[0:mid, :] = packed[mid:]
        low_ref[mid : mid + 8, :] = jnp.broadcast_to(diagonal, (8, width))

    @pl.when(parity == 0)
    def _():
        put(keep_ref, send_ref)

    @pl.when(parity != 0)
    def _():
        put(send_ref, keep_ref)


def factor(full, inv_ref):
    width = full.shape[1]
    tiles = width // 8
    sub, lane = iotas((8, width))
    work = [full[8 * t : 8 * t + 8, :] for t in range(tiles)]
    nought = jnp.where(lane < 0, 1.0, 0.0)
    for p in range(tiles):
        at = 8 * p
        inside = (lane >= at) & (lane < at + 8)
        column = [jnp.broadcast_to(work[p][:, at + j : at + j + 1], (8, width)) + nought for j in range(8)]
        a = {}
        for j in range(8):
            for i in range(j, 8):
                a[i, j] = jnp.broadcast_to(column[j][i : i + 1, :], (8, width))
        m, recip = {}, []
        for j in range(8):
            recip.append(1.0 / a[j, j])
            for i in range(j + 1, 8):
                m[i, j] = a[i, j] * recip[j]
            for i in range(j + 1, 8):
                for k in range(j + 1, i + 1):
                    a[i, k] = a[i, k] - m[i, j] * a[k, j]
        cleared = jnp.where(inside, jnp.where(lane == sub + at, 1.0, 0.0), work[p])
        pivot = []
        for j in range(8):
            r = jnp.broadcast_to(cleared[j : j + 1, :], (8, width))
            for k in range(j):
                r = r - m[j, k] * pivot[k]
            pivot.append(r)
        out = jnp.zeros((8, width), jnp.float32)
        for j in range(8):
            out = jnp.where(sub == j, pivot[j] * lax.rsqrt(a[j, j]), out)
        inv_ref[at : at + 8, :] = jnp.where(lane <= sub + at, out, 0.0)
        scaled = [pivot[j] * recip[j] for j in range(8)]
        solved = [None] * 8
        for k in reversed(range(8)):
            q = scaled[k]
            for j in range(k + 1, 8):
                q = q - m[j, k] * solved[j]
            solved[k] = q
        for t in range(p + 1, tiles):
            raw = [jnp.broadcast_to(work[t][:, at + j : at + j + 1], (8, width)) for j in range(8)]
            acc = jnp.where(inside, 0.0, work[t])
            if t == p + 1:
                w = []
                for j in range(8):
                    x = raw[j]
                    for k in range(j):
                        x = x - w[k] * m[j, k]
                    w.append(x)
                    acc = acc - x * scaled[j]
            else:
                for j in range(8):
                    acc = acc - raw[j] * solved[j]
            work[t] = acc


def finish(axis, total_nodes, mine_ref, other_ref, filt_ref, orth_hbm, proj_hbm, inv_ref, orth_ref, proj_ref, sems):
    nblocks, block, width = filt_ref.shape
    mid = width // 2
    swapped = lax.rem(lax.axis_index(axis), 2) != 0
    mine, other = mine_ref[...], other_ref[...]
    top = jnp.where(swapped, other, mine)
    low = jnp.where(swapped, mine, other)
    packed = jnp.concatenate([top[:mid], low[:mid]], 0)
    rows, cols = iotas((width, width))
    turned = packed.T
    full = jnp.where(rows >= cols, packed, turned)
    mixed = jnp.where(rows < cols, packed, jnp.where(rows > cols, turned, top[mid : mid + 1, :]))
    factor(full, inv_ref)
    inv = inv_ref[...]
    inv_r = right6(inv, 1)
    copies = []
    grown = right6(inv * math.sqrt(total_nodes), 1)
    for b in range(nblocks):
        orth_ref[b] = dot(left6(filt_ref[b]), grown, (1, 1))
        copies.append(pltpu.make_async_copy(orth_ref.at[b], orth_hbm.at[b], sems.at[b]))
        copies[b].start()
    half = dot(left6(inv), right6(mixed))
    proj_ref[...] = dot(left6(half), inv_r, (1, 1))
    copies.append(pltpu.make_async_copy(proj_ref, proj_hbm, sems.at[nblocks]))
    copies[nblocks].start()
    for copy in copies:
        copy.wait()


def shape(*dims, kind=jnp.float32):
    return jax.ShapeDtypeStruct(dims, kind)


def add_up(values, axis, stride=1):
    count = lax.axis_size(axis)
    index = lax.axis_index(axis)
    while stride < count:
        left = count // stride
        radix = next(r for r in range(2, left + 1) if left % r == 0)
        if radix == 2:
            route = [(i, i + stride if (i // stride) % 2 == 0 else i - stride) for i in range(count)]
            values = values + lax.ppermute(values, axis, route)
        else:
            place = (index // stride) % radix
            parts = [values]
            for hop in range(1, radix):
                route = []
                for i in range(count):
                    digit = (i // stride) % radix
                    route.append((i, i + ((digit - hop) % radix - digit) * stride))
                parts.append(lax.ppermute(values, axis, route))
            stacked = jnp.stack(parts)
            total = None
            for digit in range(radix):
                term = lax.dynamic_index_in_dim(stacked, (digit - place) % radix, 0, keepdims=False)
                total = term if total is None else total + term
            values = total
        stride *= radix
    return values


def swap(values, axis, start):
    count = lax.axis_size(axis)
    route = []
    for i in range(start, count - 1, 2):
        route += [(i, i + 1), (i + 1, i)]
    return lax.ppermute(values, axis, route)


def body(states, diag_blocks, couplings):
    axis = "dom"
    nodes_dev, width = states.shape
    nblocks, block, unused = diag_blocks.shape
    devices = lax.axis_size(axis)
    field = states.reshape(nblocks, block, width)
    params = pltpu.CompilerParams(vmem_limit_bytes=40 << 20)
    cross = shape(4, block, width)
    tall = shape(nblocks, block, width)
    square = shape(nblocks, block, block)
    wide = shape(nblocks, block, 3 * block, kind=jnp.bfloat16)

    def call(kernel, name, ins, outs, scratch=()):
        return pl.pallas_call(
            kernel,
            out_shape=tuple(s for s, spec in outs),
            in_specs=ins,
            out_specs=tuple(spec for s, spec in outs),
            scratch_shapes=scratch,
            compiler_params=params,
            name=name,
        )

    odd, s, d, c = call(
        lambda *refs: edge(axis, *refs),
        "edge",
        [far] * 3,
        [(cross, here), (tall, here), (square, here), (square, here)],
        [pltpu.SemaphoreType.DMA((3,))],
    )(*(pltpu.with_memory_space_constraint(x, pltpu.HBM) for x in (field, diag_blocks, couplings)))
    odd = swap(odd, axis, 1)
    even, sym, cl, ct, first, pre, onward = call(
        lambda *refs: inner(axis, *refs),
        "inner",
        [here] * 3,
        [(cross, here), (wide, here), (wide, here), (wide, here), (tall, here), (tall, here), (shape(block, width), here)],
    )(s, d, c)
    even = swap(even, axis, 0)
    piece = shape(width // 2 + 8, width)
    filtered, keep, send = call(
        lambda *refs: project(axis, *refs),
        "project",
        [here] * 9,
        [(tall, here), (piece, here), (piece, here)],
    )(s, sym, cl, ct, first, pre, onward, even, odd)
    mine = add_up(keep + swap(send, axis, 0), axis, 2)
    other = swap(mine, axis, 0)
    orthonormal, projected = call(
        lambda *refs: finish(axis, nodes_dev * devices, *refs),
        "finish",
        [here] * 3,
        [(tall, far), (shape(width, width), far)],
        [
            pltpu.VMEM((width, width), jnp.float32),
            pltpu.VMEM((nblocks, block, width), jnp.float32),
            pltpu.VMEM((width, width), jnp.float32),
            pltpu.SemaphoreType.DMA((nblocks + 1,)),
        ],
    )(mine, other, filtered)
    return orthonormal.reshape(nodes_dev, width), projected


def solution(mesh):
    in_specs = (P("dom", None), P("dom", None, None), P("dom", None, None))
    out_specs = (P("dom", None), P())
    return jax.shard_map(body, mesh=mesh, in_specs=in_specs, out_specs=out_specs, check_vma=False)
```

```python
import math

import jax
import jax.numpy as jnp
from jax import lax
from jax.experimental import pallas as pl
from jax.experimental.pallas import tpu as pltpu
from jax.sharding import PartitionSpec as P

center = 0.5
half_width = 4.0
scale = 2.0 / half_width
here = pl.BlockSpec(memory_space=pltpu.VMEM)
far = pl.BlockSpec(memory_space=pltpu.HBM)


def two(x):
    high = x.astype(jnp.bfloat16)
    return high, (x - high.astype(jnp.float32)).astype(jnp.bfloat16)


def three(x):
    high = x.astype(jnp.bfloat16)
    rest = x - high.astype(jnp.float32)
    mid = rest.astype(jnp.bfloat16)
    return high, mid, (rest - mid.astype(jnp.float32)).astype(jnp.bfloat16)


def dot(a, b, on=(1, 0)):
    return lax.dot_general(a, b, (((on[0],), (on[1],)), ((), ())), preferred_element_type=jnp.float32)


def left3(x, axis=1):
    high, low = two(x)
    return jnp.concatenate([high, high, low], axis)


def right3(x, axis=0):
    high, low = two(x)
    return jnp.concatenate([high, low, high], axis)


def left6(x, axis=1):
    high, mid, low = three(x)
    return jnp.concatenate([high, high, mid, high, low, mid], axis)


def right6(x, axis=0):
    high, mid, low = three(x)
    return jnp.concatenate([high, mid, high, low, high, mid], axis)


def iotas(shape):
    return (
        lax.broadcasted_iota(jnp.int32, shape, 0),
        lax.broadcasted_iota(jnp.int32, shape, 1),
    )


def symmetric(d):
    rows, cols = iotas(d.shape)
    return 0.5 * (d + d.T) - jnp.where(rows == cols, center, 0.0)


def leftward(s0, s1, s2, sym0, sym1, c0, c1, out_ref):
    l0, r0, r1 = left3(sym0), right3(s0), right3(s1)
    c0l = left3(c0)
    part = (dot(l0, r0) + dot(c0l, r1)) / half_width
    first1 = (dot(left3(sym1), r1) + dot(left3(c1), right3(s2)) + dot(left3(c0.T), r0)) / half_width
    out_ref[0] = s0
    out_ref[1] = part
    out_ref[2] = scale * (dot(l0, right3(part)) + dot(c0l, right3(first1))) - s0
    out_ref[3] = sym0


def rightward(s_prev, s_last, sym_last, c_prev, c_last, out_ref):
    rl = right3(s_last)
    part = (dot(left3(sym_last), rl) + dot(left3(c_prev.T), right3(s_prev))) / half_width
    turned = left3(c_last.T)
    out_ref[0] = dot(turned, rl)
    out_ref[1] = dot(turned, right3(part))
    out_ref[2] = c_last
    out_ref[3] = jnp.zeros_like(c_last)


def edge(axis, s_hbm, d_hbm, c_hbm, odd_ref, s_ref, d_ref, c_ref, sems):
    nblocks = d_hbm.shape[0]
    last = nblocks - 1
    parity = lax.rem(lax.axis_index(axis), 2)
    is_last = lax.axis_index(axis) == lax.axis_size(axis) - 1
    copies = []
    for k, (source, target) in enumerate(((s_hbm, s_ref), (d_hbm, d_ref), (c_hbm, c_ref))):
        copies.append(pltpu.make_async_copy(source, target, sems.at[k]))
    for copy in copies:
        copy.start()
    for copy in copies:
        copy.wait()

    @pl.when(is_last)
    def _():
        c_ref[last] = jnp.zeros_like(c_ref[last])

    @pl.when(parity == 0)
    def _():
        leftward(s_ref[0], s_ref[1], s_ref[2], symmetric(d_ref[0]), symmetric(d_ref[1]), c_ref[0], c_ref[1], odd_ref)

    @pl.when(parity != 0)
    def _():
        rightward(s_ref[last - 1], s_ref[last], symmetric(d_ref[last]), c_ref[last - 1], c_ref[last], odd_ref)


def inner(axis, s_ref, d_ref, c_ref, even_ref, sym_ref, cl_ref, ct_ref, first_ref, pre_ref, pass_ref):
    nblocks = d_ref.shape[0]
    last = nblocks - 1
    parity = lax.rem(lax.axis_index(axis), 2)

    @pl.when(parity != 0)
    def _():
        leftward(s_ref[0], s_ref[1], s_ref[2], symmetric(d_ref[0]), symmetric(d_ref[1]), c_ref[0], c_ref[1], even_ref)

    @pl.when(parity == 0)
    def _():
        rightward(s_ref[last - 1], s_ref[last], symmetric(d_ref[last]), c_ref[last - 1], c_ref[last], even_ref)

    s = [s_ref[b] for b in range(nblocks)]
    sr = [right3(x) for x in s]
    for b in range(nblocks):
        sym_ref[b] = left3(symmetric(d_ref[b]))
        cl_ref[b] = left3(c_ref[b])
        ct_ref[b] = left3(c_ref[b].T)
    first = []
    for b in range(nblocks):
        acc = dot(sym_ref[b], sr[b])
        if b < last:
            acc += dot(cl_ref[b], sr[b + 1])
        if b > 0:
            acc += dot(ct_ref[b - 1], sr[b - 1])
        first.append(acc / half_width)
        first_ref[b] = first[b]
    pass_ref[...] = dot(ct_ref[last], sr[last])
    fr = [right3(x) for x in first]
    for b in range(nblocks):
        acc = None
        terms = []
        if 0 < b < last:
            terms.append((sym_ref, b, b))
        if b + 1 < last:
            terms.append((cl_ref, b, b + 1))
        if b > 1:
            terms.append((ct_ref, b - 1, b - 1))
        for ref, which, operand in terms:
            term = dot(ref[which], fr[operand])
            acc = term if acc is None else acc + term
        pre_ref[b] = -s[b] if acc is None else scale * acc - s[b]


def project(axis, s_ref, sym_ref, cl_ref, ct_ref, first_ref, pre_ref, pass_ref, even_ref, odd_ref, filt_ref, keep_ref, send_ref):
    nblocks, block, unused = s_ref.shape
    last = nblocks - 1
    parity = lax.rem(lax.axis_index(axis), 2)
    right = [jnp.where(parity == 0, even_ref[k], odd_ref[k]) for k in range(4)]
    left = [jnp.where(parity == 0, odd_ref[k], even_ref[k]) for k in range(3)]
    onward = pass_ref[...]
    tail = first_ref[last] + dot(cl_ref[last], right3(right[0])) / half_width
    head = first_ref[0] + left[0] / half_width
    ahead = right[1] + onward / half_width
    back = dot(left3(left[2]), right3(s_ref[0]))
    behind = left[1] + dot(left3(left[2].T), right3(back)) / half_width
    tail_r, head_r = right3(tail), right3(head)
    filtered = [pre_ref[b] for b in range(nblocks)]
    filtered[0] += scale * (dot(sym_ref[0], head_r) + behind)
    filtered[1] += scale * dot(ct_ref[0], head_r)
    filtered[last - 1] += scale * dot(cl_ref[last - 1], tail_r)
    filtered[last] += scale * (dot(sym_ref[last], tail_r) + dot(cl_ref[last], right3(ahead)))
    beyond = right[2] + scale * (dot(left3(right[3]), right3(onward)) / half_width + dot(ct_ref[last], tail_r))
    filtered.append(beyond)
    fr = [right3(x) for x in filtered]
    both = []
    for b in range(nblocks):
        filt_ref[b] = filtered[b]
        image = 0.5 * (dot(sym_ref[b], fr[b]) + center * filtered[b]) + dot(cl_ref[b], fr[b + 1])
        both.append(jnp.concatenate([filtered[b], image], 1))
    total = None
    for b in range(nblocks):
        term = dot(left6(filtered[b], 0), right6(both[b], 0), (0, 0))
        total = term if total is None else total + term
    width = filtered[0].shape[1]
    correlation, half = total[:, :width], total[:, width:]
    mixed = half + half.T
    rows, cols = iotas((width, width))
    packed = jnp.where(rows >= cols, correlation, mixed)
    diagonal = jnp.sum(jnp.where(rows == cols, mixed, 0.0), axis=0, keepdims=True)
    mid = width // 2

    def put(top_ref, low_ref):
        top_ref[0:mid, :] = packed[:mid]
        top_ref[mid : mid + 8, :] = jnp.broadcast_to(diagonal, (8, width))
        low_ref[0:mid, :] = packed[mid:]
        low_ref[mid : mid + 8, :] = jnp.broadcast_to(diagonal, (8, width))

    @pl.when(parity == 0)
    def _():
        put(keep_ref, send_ref)

    @pl.when(parity != 0)
    def _():
        put(send_ref, keep_ref)


def factor(full, inv_ref):
    width = full.shape[1]
    tiles = width // 8
    sub, lane = iotas((8, width))
    work = [full[8 * t : 8 * t + 8, :] for t in range(tiles)]
    nought = jnp.where(lane < 0, 1.0, 0.0)
    for p in range(tiles):
        at = 8 * p
        inside = (lane >= at) & (lane < at + 8)
        column = [jnp.broadcast_to(work[p][:, at + j : at + j + 1], (8, width)) + nought for j in range(8)]
        a = {}
        for j in range(8):
            for i in range(j, 8):
                a[i, j] = jnp.broadcast_to(column[j][i : i + 1, :], (8, width))
        m, recip = {}, []
        for j in range(8):
            recip.append(1.0 / a[j, j])
            for i in range(j + 1, 8):
                m[i, j] = a[i, j] * recip[j]
            for i in range(j + 1, 8):
                for k in range(j + 1, i + 1):
                    a[i, k] = a[i, k] - m[i, j] * a[k, j]
        cleared = jnp.where(inside, jnp.where(lane == sub + at, 1.0, 0.0), work[p])
        pivot = []
        for j in range(8):
            r = jnp.broadcast_to(cleared[j : j + 1, :], (8, width))
            for k in range(j):
                r = r - m[j, k] * pivot[k]
            pivot.append(r)
        out = jnp.zeros((8, width), jnp.float32)
        for j in range(8):
            out = jnp.where(sub == j, pivot[j] * lax.rsqrt(a[j, j]), out)
        inv_ref[at : at + 8, :] = jnp.where(lane <= sub + at, out, 0.0)
        scaled = [pivot[j] * recip[j] for j in range(8)]
        solved = [None] * 8
        for k in reversed(range(8)):
            q = scaled[k]
            for j in range(k + 1, 8):
                q = q - m[j, k] * solved[j]
            solved[k] = q
        for t in range(p + 1, tiles):
            raw = [jnp.broadcast_to(work[t][:, at + j : at + j + 1], (8, width)) for j in range(8)]
            acc = jnp.where(inside, 0.0, work[t])
            if t == p + 1:
                w = []
                for j in range(8):
                    x = raw[j]
                    for k in range(j):
                        x = x - w[k] * m[j, k]
                    w.append(x)
                    acc = acc - x * scaled[j]
            else:
                for j in range(8):
                    acc = acc - raw[j] * solved[j]
            work[t] = acc


def finish(axis, total_nodes, mine_ref, other_ref, filt_ref, orth_hbm, proj_hbm, inv_ref, orth_ref, proj_ref, sems):
    nblocks, block, width = filt_ref.shape
    mid = width // 2
    swapped = lax.rem(lax.axis_index(axis), 2) != 0
    mine, other = mine_ref[...], other_ref[...]
    top = jnp.where(swapped, other, mine)
    low = jnp.where(swapped, mine, other)
    packed = jnp.concatenate([top[:mid], low[:mid]], 0)
    rows, cols = iotas((width, width))
    turned = packed.T
    full = jnp.where(rows >= cols, packed, turned)
    mixed = jnp.where(rows < cols, packed, jnp.where(rows > cols, turned, top[mid : mid + 1, :]))
    factor(full, inv_ref)
    inv = inv_ref[...]
    inv_r = right6(inv, 1)
    copies = []
    grown = right6(inv * math.sqrt(total_nodes), 1)
    for b in range(nblocks):
        orth_ref[b] = dot(left6(filt_ref[b]), grown, (1, 1))
        copies.append(pltpu.make_async_copy(orth_ref.at[b], orth_hbm.at[b], sems.at[b]))
        copies[b].start()
    half = dot(left6(inv), right6(mixed))
    proj_ref[...] = dot(left6(half), inv_r, (1, 1))
    copies.append(pltpu.make_async_copy(proj_ref, proj_hbm, sems.at[nblocks]))
    copies[nblocks].start()
    for copy in copies:
        copy.wait()


def shape(*dims, kind=jnp.float32):
    return jax.ShapeDtypeStruct(dims, kind)


def add_up(values, axis, stride=1):
    count = lax.axis_size(axis)
    index = lax.axis_index(axis)
    while stride < count:
        left = count // stride
        radix = 4 if left % 4 == 0 else next(r for r in range(2, left + 1) if left % r == 0)

        def route(partner):
            digits = [(i // stride) % radix for i in range(count)]
            return [(i, i + (partner(k) - k) * stride) for i, k in enumerate(digits)]

        if radix in (2, 4):
            parts = [values]
            for flip in range(1, radix):
                parts.append(lax.ppermute(values, axis, route(lambda k: k ^ flip)))
            while len(parts) > 1:
                parts = [a + b for a, b in zip(parts[::2], parts[1::2])]
            values = parts[0]
        else:
            place = (index // stride) % radix
            parts = [values]
            for hop in range(1, radix):
                parts.append(lax.ppermute(values, axis, route(lambda k: (k - hop) % radix)))
            stacked = jnp.stack(parts)
            total = None
            for digit in range(radix):
                term = lax.dynamic_index_in_dim(stacked, (digit - place) % radix, 0, keepdims=False)
                total = term if total is None else total + term
            values = total
        stride *= radix
    return values


def swap(values, axis, start):
    count = lax.axis_size(axis)
    route = []
    for i in range(start, count - 1, 2):
        route += [(i, i + 1), (i + 1, i)]
    return lax.ppermute(values, axis, route)


def body(states, diag_blocks, couplings):
    axis = "dom"
    nodes_dev, width = states.shape
    nblocks, block, unused = diag_blocks.shape
    devices = lax.axis_size(axis)
    field = states.reshape(nblocks, block, width)
    params = pltpu.CompilerParams(vmem_limit_bytes=40 << 20)
    cross = shape(4, block, width)
    tall = shape(nblocks, block, width)
    square = shape(nblocks, block, block)
    wide = shape(nblocks, block, 3 * block, kind=jnp.bfloat16)

    def call(kernel, name, ins, outs, scratch=()):
        return pl.pallas_call(
            kernel,
            out_shape=tuple(s for s, spec in outs),
            in_specs=ins,
            out_specs=tuple(spec for s, spec in outs),
            scratch_shapes=scratch,
            compiler_params=params,
            name=name,
        )

    odd, s, d, c = call(
        lambda *refs: edge(axis, *refs),
        "edge",
        [far] * 3,
        [(cross, here), (tall, here), (square, here), (square, here)],
        [pltpu.SemaphoreType.DMA((3,))],
    )(*(pltpu.with_memory_space_constraint(x, pltpu.HBM) for x in (field, diag_blocks, couplings)))
    odd = swap(odd, axis, 1)
    even, sym, cl, ct, first, pre, onward = call(
        lambda *refs: inner(axis, *refs),
        "inner",
        [here] * 3,
        [(cross, here), (wide, here), (wide, here), (wide, here), (tall, here), (tall, here), (shape(block, width), here)],
    )(s, d, c)
    even = swap(even, axis, 0)
    piece = shape(width // 2 + 8, width)
    filtered, keep, send = call(
        lambda *refs: project(axis, *refs),
        "project",
        [here] * 9,
        [(tall, here), (piece, here), (piece, here)],
    )(s, sym, cl, ct, first, pre, onward, even, odd)
    mine = add_up(keep + swap(send, axis, 0), axis, 2)
    other = swap(mine, axis, 0)
    orthonormal, projected = call(
        lambda *refs: finish(axis, nodes_dev * devices, *refs),
        "finish",
        [here] * 3,
        [(tall, far), (shape(width, width), far)],
        [
            pltpu.VMEM((width, width), jnp.float32),
            pltpu.VMEM((nblocks, block, width), jnp.float32),
            pltpu.VMEM((width, width), jnp.float32),
            pltpu.SemaphoreType.DMA((nblocks + 1,)),
        ],
    )(mine, other, filtered)
    return orthonormal.reshape(nodes_dev, width), projected


def solution(mesh):
    in_specs = (P("dom", None), P("dom", None, None), P("dom", None, None))
    out_specs = (P("dom", None), P())
    return jax.shard_map(body, mesh=mesh, in_specs=in_specs, out_specs=out_specs, check_vma=False)
```

```python
import math

import jax
import jax.numpy as jnp
from jax import lax
from jax.experimental import pallas as pl
from jax.experimental.pallas import tpu as pltpu
from jax.sharding import PartitionSpec as P

center = 0.5
half_width = 4.0
scale = 2.0 / half_width
here = pl.BlockSpec(memory_space=pltpu.VMEM)
far = pl.BlockSpec(memory_space=pltpu.HBM)


def two(x):
    high = x.astype(jnp.bfloat16)
    return high, (x - high.astype(jnp.float32)).astype(jnp.bfloat16)


def three(x):
    high = x.astype(jnp.bfloat16)
    rest = x - high.astype(jnp.float32)
    mid = rest.astype(jnp.bfloat16)
    return high, mid, (rest - mid.astype(jnp.float32)).astype(jnp.bfloat16)


def dot(a, b, on=(1, 0)):
    return lax.dot_general(a, b, (((on[0],), (on[1],)), ((), ())), preferred_element_type=jnp.float32)


def left3(x, axis=1):
    high, low = two(x)
    return jnp.concatenate([high, high, low], axis)


def right3(x, axis=0):
    high, low = two(x)
    return jnp.concatenate([high, low, high], axis)


def left6(x, axis=1):
    high, mid, low = three(x)
    return jnp.concatenate([high, high, mid, high, low, mid], axis)


def right6(x, axis=0):
    high, mid, low = three(x)
    return jnp.concatenate([high, mid, high, low, high, mid], axis)


def iotas(shape):
    return (
        lax.broadcasted_iota(jnp.int32, shape, 0),
        lax.broadcasted_iota(jnp.int32, shape, 1),
    )


def symmetric(d):
    rows, cols = iotas(d.shape)
    return 0.5 * (d + d.T) - jnp.where(rows == cols, center, 0.0)


def pack(sym):
    block = sym.shape[0]
    mid = block // 2
    rows, cols = iotas((mid, block))
    top, low = sym[:mid], sym[mid:]
    body = jnp.where((cols >= mid) | (rows >= cols), top, pltpu.roll(low, mid, 1))
    diagonal = jnp.sum(jnp.where(cols == rows + mid, low, 0.0), axis=0, keepdims=True)
    return jnp.concatenate([body, jnp.broadcast_to(diagonal, (8, block))], 0)


def unpack(packed):
    block = packed.shape[1]
    mid = block // 2
    rows, cols = iotas((mid, block))
    body, diagonal = packed[:mid], packed[mid : mid + 1]
    top = jnp.where((cols >= mid) | (rows > cols), body, 0.0)
    low = pltpu.roll(jnp.where((cols < mid) & (rows < cols), body, 0.0), mid, 1)
    part = jnp.concatenate([top, low], 0)
    middle = jnp.concatenate([jnp.where(rows == cols, body, 0.0), jnp.where(cols == rows + mid, diagonal, 0.0)], 0)
    return part + part.T + middle


def leftward(s0, s1, s2, sym0, sym1, c0, c1, out_ref, more_ref):
    block = s0.shape[0]
    l0, r0, r1 = left3(sym0), right3(s0), right3(s1)
    c0l = left3(c0)
    part = (dot(l0, r0) + dot(c0l, r1)) / half_width
    first1 = (dot(left3(sym1), r1) + dot(left3(c1), right3(s2)) + dot(left3(c0.T), r0)) / half_width
    out_ref[0:block] = s0
    out_ref[block : 2 * block] = part
    out_ref[2 * block : 2 * block + block // 2 + 8] = pack(sym0)
    more_ref[...] = scale * (dot(l0, right3(part)) + dot(c0l, right3(first1))) - s0


def rightward(s_prev, s_last, sym_last, c_prev, c_last, out_ref, more_ref):
    block = s_last.shape[0]
    rl = right3(s_last)
    part = (dot(left3(sym_last), rl) + dot(left3(c_prev.T), right3(s_prev))) / half_width
    turned = left3(c_last.T)
    out_ref[0:block] = dot(turned, rl)
    out_ref[block : 2 * block] = dot(turned, right3(part))
    out_ref[2 * block : 2 * block + block // 2 + 8] = pack(dot(turned, right3(c_last)))
    more_ref[...] = jnp.zeros_like(c_last)


def edge(axis, s_hbm, d_hbm, c_hbm, odd_ref, s_ref, d_ref, c_ref, sems):
    nblocks = d_hbm.shape[0]
    last = nblocks - 1
    parity = lax.rem(lax.axis_index(axis), 2)
    block = s_hbm.shape[1]
    swap_ref, more_ref = odd_ref.at[: odd_ref.shape[0] - block], odd_ref.at[odd_ref.shape[0] - block :]
    is_last = lax.axis_index(axis) == lax.axis_size(axis) - 1
    copies = []
    for k, (source, target) in enumerate(((s_hbm, s_ref), (d_hbm, d_ref), (c_hbm, c_ref))):
        copies.append(pltpu.make_async_copy(source, target, sems.at[k]))
    for copy in copies:
        copy.start()
    for copy in copies:
        copy.wait()

    @pl.when(is_last)
    def _():
        c_ref[last] = jnp.zeros_like(c_ref[last])

    @pl.when(parity == 0)
    def _():
        leftward(s_ref[0], s_ref[1], s_ref[2], symmetric(d_ref[0]), symmetric(d_ref[1]), c_ref[0], c_ref[1], swap_ref, more_ref)

    @pl.when(parity != 0)
    def _():
        rightward(s_ref[last - 1], s_ref[last], symmetric(d_ref[last]), c_ref[last - 1], c_ref[last], swap_ref, more_ref)


def inner(axis, s_ref, d_ref, c_ref, even_ref, sym_ref, cl_ref, ct_ref, first_ref, pre_ref, pass_ref):
    nblocks = d_ref.shape[0]
    last = nblocks - 1
    block = s_ref.shape[1]
    parity = lax.rem(lax.axis_index(axis), 2)
    swap_ref, more_ref = even_ref.at[: even_ref.shape[0] - block], even_ref.at[even_ref.shape[0] - block :]

    @pl.when(parity != 0)
    def _():
        leftward(s_ref[0], s_ref[1], s_ref[2], symmetric(d_ref[0]), symmetric(d_ref[1]), c_ref[0], c_ref[1], swap_ref, more_ref)

    @pl.when(parity == 0)
    def _():
        rightward(s_ref[last - 1], s_ref[last], symmetric(d_ref[last]), c_ref[last - 1], c_ref[last], swap_ref, more_ref)

    s = [s_ref[b] for b in range(nblocks)]
    sr = [right3(x) for x in s]
    for b in range(nblocks):
        sym_ref[b] = left3(symmetric(d_ref[b]))
        cl_ref[b] = left3(c_ref[b])
        ct_ref[b] = left3(c_ref[b].T)
    first = []
    for b in range(nblocks):
        acc = dot(sym_ref[b], sr[b])
        if b < last:
            acc += dot(cl_ref[b], sr[b + 1])
        if b > 0:
            acc += dot(ct_ref[b - 1], sr[b - 1])
        first.append(acc / half_width)
        first_ref[b] = first[b]
    pass_ref[...] = dot(ct_ref[last], sr[last])
    fr = [right3(x) for x in first]
    for b in range(nblocks):
        acc = None
        terms = []
        if 0 < b < last:
            terms.append((sym_ref, b, b))
        if b + 1 < last:
            terms.append((cl_ref, b, b + 1))
        if b > 1:
            terms.append((ct_ref, b - 1, b - 1))
        for ref, which, operand in terms:
            term = dot(ref[which], fr[operand])
            acc = term if acc is None else acc + term
        pre_ref[b] = -s[b] if acc is None else scale * acc - s[b]


def project(axis, s_ref, sym_ref, cl_ref, ct_ref, first_ref, pre_ref, pass_ref, even_ref, odd_ref, filt_ref, keep_ref, send_ref):
    nblocks, block, _ = s_ref.shape
    last = nblocks - 1
    parity = lax.rem(lax.axis_index(axis), 2)
    rows = odd_ref.shape[0] - block
    cuts = ((0, block), (block, 2 * block), (2 * block, rows))
    right = [jnp.where(parity == 0, even_ref[a:b], odd_ref[a:b]) for a, b in cuts]
    left = [jnp.where(parity == 0, odd_ref[a:b], even_ref[a:b]) for a, b in cuts]
    other = jnp.where(parity == 0, even_ref[rows:], odd_ref[rows:])
    onward = pass_ref[...]
    tail = first_ref[last] + dot(cl_ref[last], right3(right[0])) / half_width
    head = first_ref[0] + left[0] / half_width
    ahead = right[1] + onward / half_width
    behind = left[1] + dot(left3(unpack(left[2])), right3(s_ref[0])) / half_width
    tail_r, head_r = right3(tail), right3(head)
    filtered = [pre_ref[b] for b in range(nblocks)]
    filtered[0] += scale * (dot(sym_ref[0], head_r) + behind)
    filtered[1] += scale * dot(ct_ref[0], head_r)
    filtered[last - 1] += scale * dot(cl_ref[last - 1], tail_r)
    filtered[last] += scale * (dot(sym_ref[last], tail_r) + dot(cl_ref[last], right3(ahead)))
    beyond = other + scale * (dot(left3(unpack(right[2])), right3(onward)) / half_width + dot(ct_ref[last], tail_r))
    filtered.append(beyond)
    fr = [right3(x) for x in filtered]
    both = []
    for b in range(nblocks):
        filt_ref[b] = filtered[b]
        image = 0.5 * (dot(sym_ref[b], fr[b]) + center * filtered[b]) + dot(cl_ref[b], fr[b + 1])
        both.append(jnp.concatenate([filtered[b], image], 1))
    total = None
    for b in range(nblocks):
        term = dot(left6(filtered[b], 0), right6(both[b], 0), (0, 0))
        total = term if total is None else total + term
    width = filtered[0].shape[1]
    correlation, half = total[:, :width], total[:, width:]
    mixed = half + half.T
    rows, cols = iotas((width, width))
    packed = jnp.where(rows >= cols, correlation, mixed)
    diagonal = jnp.sum(jnp.where(rows == cols, mixed, 0.0), axis=0, keepdims=True)
    mid = width // 2

    def put(top_ref, low_ref):
        top_ref[0:mid, :] = packed[:mid]
        top_ref[mid : mid + 8, :] = jnp.broadcast_to(diagonal, (8, width))
        low_ref[0:mid, :] = packed[mid:]
        low_ref[mid : mid + 8, :] = jnp.broadcast_to(diagonal, (8, width))

    @pl.when(parity == 0)
    def _():
        put(keep_ref, send_ref)

    @pl.when(parity != 0)
    def _():
        put(send_ref, keep_ref)


def factor(full, inv_ref, group=8):
    width = full.shape[1]
    tiles = width // 8
    sub, lane = iotas((8, width))
    nought = jnp.where(lane < 0, 1.0, 0.0)

    def along(x, column):
        return jnp.broadcast_to(x[:, column : column + 1], (8, width))

    def down(x, row):
        return jnp.broadcast_to(x[row : row + 1, :], (8, width))

    work = [full[8 * t : 8 * t + 8, :] for t in range(tiles)]
    col, done = [], []
    for p in range(tiles):
        at = 8 * p
        start = p - p % group
        end = min(tiles, start + group)
        inside = (lane >= at) & (lane < at + 8)
        if p == start:
            done = []
            col = [along(work[p], at + j) + nought for j in range(8)]
        raw = {(t, j): along(work[t], at + j) for j in range(8) for t in range(p + 1, end)}
        diagonal, recip, m = [], [], {}
        for j in range(8):
            diagonal.append(down(col[j], j))
            recip.append(1.0 / diagonal[j])
            for k in range(j + 1, 8):
                m[k, j] = down(col[j], k) * recip[j]
                col[k] = col[k] - col[j] * m[k, j]
        coming = []
        if p + 1 < end:
            w = [raw[p + 1, j] + nought for j in range(8)]
            coming = [along(work[p + 1], at + 8 + k) + nought for k in range(8)]
            for j in range(8):
                for k in range(j + 1, 8):
                    w[k] = w[k] - w[j] * m[k, j]
                for k in range(8):
                    coming[k] = coming[k] - w[j] * (down(w[j], k) * recip[j])
        cleared = jnp.where(inside, jnp.where(lane == sub + at, 1.0, 0.0), work[p])
        pivot = []
        for j in range(8):
            r = down(cleared, j)
            for k in range(j):
                r = r - m[j, k] * pivot[k]
            pivot.append(r)
        out = jnp.zeros((8, width), jnp.float32)
        for j in range(8):
            out = jnp.where(sub == j, pivot[j] * lax.rsqrt(diagonal[j]), out)
        inv_ref[at : at + 8, :] = jnp.where(lane <= sub + at, out, 0.0)
        done.append(jnp.where((lane > sub + at) & (lane < 8 * end), 0.0, out))
        solved = [None] * 8
        for k in reversed(range(8)):
            q = pivot[k] * recip[k]
            for j in reversed(range(k + 1, 8)):
                q = q - m[j, k] * solved[j]
            solved[k] = q
        for t in range(p + 1, end):
            acc = jnp.where(inside, 0.0, work[t])
            for j in reversed(range(8)):
                acc = acc - raw[t, j] * solved[j]
            work[t] = acc
        col = coming
        if p + 1 == end < tiles:
            rows = jnp.concatenate(done, 0)
            update = dot(left6(rows, 0), right6(rows, 0), (0, 0))
            for t in range(end, tiles):
                kept = jnp.where((lane >= 8 * start) & (lane < 8 * end), 0.0, work[t])
                work[t] = kept - update[8 * t : 8 * t + 8]


def finish(axis, total_nodes, mine_ref, other_ref, filt_ref, orth_hbm, proj_hbm, inv_ref, orth_ref, proj_ref, sems):
    nblocks, _, width = filt_ref.shape
    mid = width // 2
    swapped = lax.rem(lax.axis_index(axis), 2) != 0
    mine, other = mine_ref[...], other_ref[...]
    top = jnp.where(swapped, other, mine)
    low = jnp.where(swapped, mine, other)
    packed = jnp.concatenate([top[:mid], low[:mid]], 0)
    rows, cols = iotas((width, width))
    turned = packed.T
    full = jnp.where(rows >= cols, packed, turned)
    mixed = jnp.where(rows < cols, packed, jnp.where(rows > cols, turned, top[mid : mid + 1, :]))
    factor(full, inv_ref)
    inv = inv_ref[...]
    inv_r = right6(inv, 1)
    copies = []
    grown = right6(inv * math.sqrt(total_nodes), 1)
    for b in range(nblocks):
        orth_ref[b] = dot(left6(filt_ref[b]), grown, (1, 1))
        copies.append(pltpu.make_async_copy(orth_ref.at[b], orth_hbm.at[b], sems.at[b]))
        copies[b].start()
    half = dot(left6(inv), right6(mixed))
    proj_ref[...] = dot(left6(half), inv_r, (1, 1))
    copies.append(pltpu.make_async_copy(proj_ref, proj_hbm, sems.at[nblocks]))
    copies[nblocks].start()
    for copy in copies:
        copy.wait()


def shape(*dims, kind=jnp.float32):
    return jax.ShapeDtypeStruct(dims, kind)


def add_up(values, axis, stride=1):
    count = lax.axis_size(axis)
    index = lax.axis_index(axis)
    while stride < count:
        left = count // stride
        radix = 4 if left % 4 == 0 else next(r for r in range(2, left + 1) if left % r == 0)

        def route(partner):
            digits = [(i // stride) % radix for i in range(count)]
            return [(i, i + (partner(k) - k) * stride) for i, k in enumerate(digits)]

        if radix in (2, 4):
            parts = [values]
            for flip in range(1, radix):
                parts.append(lax.ppermute(values, axis, route(lambda k: k ^ flip)))
            while len(parts) > 1:
                parts = [a + b for a, b in zip(parts[::2], parts[1::2])]
            values = parts[0]
        else:
            place = (index // stride) % radix
            parts = [values]
            for hop in range(1, radix):
                parts.append(lax.ppermute(values, axis, route(lambda k: (k - hop) % radix)))
            stacked = jnp.stack(parts)
            total = None
            for digit in range(radix):
                term = lax.dynamic_index_in_dim(stacked, (digit - place) % radix, 0, keepdims=False)
                total = term if total is None else total + term
            values = total
        stride *= radix
    return values


def swap(values, axis, start):
    count = lax.axis_size(axis)
    route = []
    for i in range(start, count - 1, 2):
        route += [(i, i + 1), (i + 1, i)]
    return lax.ppermute(values, axis, route)


def body(states, diag_blocks, couplings):
    axis = "dom"
    nodes_dev, width = states.shape
    nblocks, block, _ = diag_blocks.shape
    devices = lax.axis_size(axis)
    field = states.reshape(nblocks, block, width)
    params = pltpu.CompilerParams(vmem_limit_bytes=40 << 20)
    cross = shape(3 * block + block // 2 + 8, width)
    tall = shape(nblocks, block, width)
    square = shape(nblocks, block, block)
    wide = shape(nblocks, block, 3 * block, kind=jnp.bfloat16)

    def call(kernel, ins, outs, scratch=()):
        return pl.pallas_call(
            kernel,
            out_shape=tuple(s for s, spec in outs),
            in_specs=ins,
            out_specs=tuple(spec for s, spec in outs),
            scratch_shapes=scratch,
            compiler_params=params,
        )

    odd, s, d, c = call(
        lambda *refs: edge(axis, *refs),
        [far] * 3,
        [(cross, here), (tall, here), (square, here), (square, here)],
        [pltpu.SemaphoreType.DMA((3,))],
    )(*(pltpu.with_memory_space_constraint(x, pltpu.HBM) for x in (field, diag_blocks, couplings)))
    odd = swap(odd, axis, 1)
    even, sym, cl, ct, first, pre, onward = call(
        lambda *refs: inner(axis, *refs),
        [here] * 3,
        [(cross, here), (wide, here), (wide, here), (wide, here), (tall, here), (tall, here), (shape(block, width), here)],
    )(s, d, c)
    even = swap(even, axis, 0)
    piece = shape(width // 2 + 8, width)
    filtered, keep, send = call(
        lambda *refs: project(axis, *refs), [here] * 9, [(tall, here), (piece, here), (piece, here)]
    )(s, sym, cl, ct, first, pre, onward, even, odd)
    mine = add_up(keep + swap(send, axis, 0), axis, 2)
    other = swap(mine, axis, 0)
    orthonormal, projected = call(
        lambda *refs: finish(axis, nodes_dev * devices, *refs),
        [here] * 3,
        [(tall, far), (shape(width, width), far)],
        [
            pltpu.VMEM((width, width), jnp.float32),
            pltpu.VMEM((nblocks, block, width), jnp.float32),
            pltpu.VMEM((width, width), jnp.float32),
            pltpu.SemaphoreType.DMA((nblocks + 1,)),
        ],
    )(mine, other, filtered)
    return orthonormal.reshape(nodes_dev, width), projected


def solution(mesh):
    in_specs = (P("dom", None), P("dom", None, None), P("dom", None, None))
    out_specs = (P("dom", None), P())

    return jax.shard_map(body, mesh=mesh, in_specs=in_specs, out_specs=out_specs, check_vma=False)
```

```python
import math

import jax
import jax.numpy as jnp
from jax import lax
from jax.experimental import pallas as pl
from jax.experimental.pallas import tpu as pltpu
from jax.sharding import PartitionSpec as P

center = 0.5
half_width = 4.0
scale = 2.0 / half_width
here = pl.BlockSpec(memory_space=pltpu.VMEM)
far = pl.BlockSpec(memory_space=pltpu.HBM)


def two(x):
    high = x.astype(jnp.bfloat16)
    return high, (x - high.astype(jnp.float32)).astype(jnp.bfloat16)


def three(x):
    high = x.astype(jnp.bfloat16)
    rest = x - high.astype(jnp.float32)
    mid = rest.astype(jnp.bfloat16)
    return high, mid, (rest - mid.astype(jnp.float32)).astype(jnp.bfloat16)


def dot(a, b, on=(1, 0)):
    return lax.dot_general(a, b, (((on[0],), (on[1],)), ((), ())), preferred_element_type=jnp.float32)


def left3(x, axis=1):
    high, low = two(x)
    return jnp.concatenate([high, high, low], axis)


def right3(x, axis=0):
    high, low = two(x)
    return jnp.concatenate([high, low, high], axis)


def left6(x, axis=1):
    high, mid, low = three(x)
    return jnp.concatenate([high, high, mid, high, low, mid], axis)


def right6(x, axis=0):
    high, mid, low = three(x)
    return jnp.concatenate([high, mid, high, low, high, mid], axis)


def beside(a, b):
    return jnp.concatenate([a, b], 1)


def stack(a, b):
    return jnp.concatenate([a, b], 0)


def iotas(shape):
    return (
        lax.broadcasted_iota(jnp.int32, shape, 0),
        lax.broadcasted_iota(jnp.int32, shape, 1),
    )


def symmetric(d):
    rows, cols = iotas(d.shape)
    return 0.5 * (d + d.T) - jnp.where(rows == cols, center, 0.0)


def pack(sym):
    block = sym.shape[0]
    mid = block // 2
    rows, cols = iotas((mid, block))
    top, low = sym[:mid], sym[mid:]
    body = jnp.where((cols >= mid) | (rows >= cols), top, pltpu.roll(low, mid, 1))
    diagonal = jnp.sum(jnp.where(cols == rows + mid, low, 0.0), axis=0, keepdims=True)
    return jnp.concatenate([body, jnp.broadcast_to(diagonal, (8, block))], 0)


def unpack(packed):
    block = packed.shape[1]
    mid = block // 2
    rows, cols = iotas((mid, block))
    body, diagonal = packed[:mid], packed[mid : mid + 1]
    top = jnp.where((cols >= mid) | (rows > cols), body, 0.0)
    low = pltpu.roll(jnp.where((cols < mid) & (rows < cols), body, 0.0), mid, 1)
    part = jnp.concatenate([top, low], 0)
    middle = jnp.concatenate([jnp.where(rows == cols, body, 0.0), jnp.where(cols == rows + mid, diagonal, 0.0)], 0)
    return part + part.T + middle


def leftward(s0, s1, s2, sym0, sym1, c0, c1, out_ref, more_ref):
    block = s0.shape[0]
    l0, r0, r1 = left3(sym0), right3(s0), right3(s1)
    c0l = left3(c0)
    part = (dot(l0, r0) + dot(c0l, r1)) / half_width
    first1 = (dot(left3(sym1), r1) + dot(left3(c1), right3(s2)) + dot(left3(c0.T), r0)) / half_width
    out_ref[0:block] = s0
    out_ref[block : 2 * block] = part
    out_ref[2 * block : 2 * block + block // 2 + 8] = pack(sym0)
    more_ref[...] = scale * (dot(l0, right3(part)) + dot(c0l, right3(first1))) - s0


def rightward(s_prev, s_last, sym_last, c_prev, c_last, out_ref, more_ref):
    block = s_last.shape[0]
    rl = right3(s_last)
    part = (dot(left3(sym_last), rl) + dot(left3(c_prev.T), right3(s_prev))) / half_width
    turned = left3(c_last.T)
    out_ref[0:block] = dot(turned, rl)
    out_ref[block : 2 * block] = dot(turned, right3(part))
    out_ref[2 * block : 2 * block + block // 2 + 8] = pack(dot(turned, right3(c_last)))
    more_ref[...] = jnp.zeros_like(c_last)


def edge(axis, s_hbm, d_hbm, c_hbm, odd_ref, s_ref, d_ref, c_ref, sems):
    nblocks = d_hbm.shape[0]
    last = nblocks - 1
    parity = lax.rem(lax.axis_index(axis), 2)
    block = s_hbm.shape[1]
    swap_ref, more_ref = odd_ref.at[: odd_ref.shape[0] - block], odd_ref.at[odd_ref.shape[0] - block :]
    is_last = lax.axis_index(axis) == lax.axis_size(axis) - 1
    copies = []
    for k, (source, target) in enumerate(((s_hbm, s_ref), (d_hbm, d_ref), (c_hbm, c_ref))):
        copies.append(pltpu.make_async_copy(source, target, sems.at[k]))
    for copy in copies:
        copy.start()
    for copy in copies:
        copy.wait()

    @pl.when(is_last)
    def _():
        c_ref[last] = jnp.zeros_like(c_ref[last])

    @pl.when(parity == 0)
    def _():
        leftward(s_ref[0], s_ref[1], s_ref[2], symmetric(d_ref[0]), symmetric(d_ref[1]), c_ref[0], c_ref[1], swap_ref, more_ref)

    @pl.when(parity != 0)
    def _():
        rightward(s_ref[last - 1], s_ref[last], symmetric(d_ref[last]), c_ref[last - 1], c_ref[last], swap_ref, more_ref)


def inner(axis, s_ref, d_ref, c_ref, even_ref, sym_ref, cl_ref, ct_ref, first_ref, pre_ref, pass_ref):
    nblocks = d_ref.shape[0]
    last = nblocks - 1
    block = s_ref.shape[1]
    parity = lax.rem(lax.axis_index(axis), 2)
    swap_ref, more_ref = even_ref.at[: even_ref.shape[0] - block], even_ref.at[even_ref.shape[0] - block :]

    @pl.when(parity != 0)
    def _():
        leftward(s_ref[0], s_ref[1], s_ref[2], symmetric(d_ref[0]), symmetric(d_ref[1]), c_ref[0], c_ref[1], swap_ref, more_ref)

    @pl.when(parity == 0)
    def _():
        rightward(s_ref[last - 1], s_ref[last], symmetric(d_ref[last]), c_ref[last - 1], c_ref[last], swap_ref, more_ref)

    s = [s_ref[b] for b in range(nblocks)]
    sr = [right3(x) for x in s]
    for b in range(nblocks):
        sym_ref[b] = left3(symmetric(d_ref[b]))
        cl_ref[b] = left3(c_ref[b])
        ct_ref[b] = left3(c_ref[b].T)
    first = []
    for b in range(nblocks):
        acc = dot(sym_ref[b], sr[b])
        if b < last:
            acc += dot(cl_ref[b], sr[b + 1])
        if b > 0:
            acc += dot(ct_ref[b - 1], sr[b - 1])
        first.append(acc / half_width)
        first_ref[b] = first[b]
    pass_ref[...] = dot(ct_ref[last], sr[last])
    fr = [right3(x) for x in first]
    for b in range(nblocks):
        acc = None
        terms = []
        if 0 < b < last:
            terms.append((sym_ref, b, b))
        if b + 1 < last:
            terms.append((cl_ref, b, b + 1))
        if b > 1:
            terms.append((ct_ref, b - 1, b - 1))
        for ref, which, operand in terms:
            term = dot(ref[which], fr[operand])
            acc = term if acc is None else acc + term
        pre_ref[b] = -s[b] if acc is None else scale * acc - s[b]


def project(axis, s_ref, sym_ref, cl_ref, ct_ref, first_ref, pre_ref, pass_ref, even_ref, odd_ref, filt_ref, keep_ref, send_ref):
    nblocks, block, _ = s_ref.shape
    last = nblocks - 1
    parity = lax.rem(lax.axis_index(axis), 2)
    rows = odd_ref.shape[0] - block
    cuts = ((0, block), (block, 2 * block), (2 * block, rows))
    right = [jnp.where(parity == 0, even_ref[a:b], odd_ref[a:b]) for a, b in cuts]
    left = [jnp.where(parity == 0, odd_ref[a:b], even_ref[a:b]) for a, b in cuts]
    other = jnp.where(parity == 0, even_ref[rows:], odd_ref[rows:])
    onward = pass_ref[...]
    tail = first_ref[last] + dot(cl_ref[last], right3(right[0])) / half_width
    head = first_ref[0] + left[0] / half_width
    ahead = right[1] + onward / half_width
    behind = left[1] + dot(left3(unpack(left[2])), right3(s_ref[0])) / half_width
    tail_r, head_r = right3(tail), right3(head)
    filtered = [pre_ref[b] for b in range(nblocks)]
    filtered[0] += scale * (dot(sym_ref[0], head_r) + behind)
    filtered[1] += scale * dot(ct_ref[0], head_r)
    filtered[last - 1] += scale * dot(cl_ref[last - 1], tail_r)
    filtered[last] += scale * dot(beside(sym_ref[last], cl_ref[last]), stack(tail_r, right3(ahead)))
    beyond = other + scale * (dot(left3(unpack(right[2])), right3(onward)) / half_width + dot(ct_ref[last], tail_r))
    filtered.append(beyond)
    fr = [right3(x) for x in filtered]
    both = []
    for b in range(nblocks):
        filt_ref[b] = filtered[b]
        image = dot(beside(sym_ref[b] * 0.5, cl_ref[b]), stack(fr[b], fr[b + 1])) + 0.5 * center * filtered[b]
        both.append(jnp.concatenate([filtered[b], image], 1))
    total = None
    for b in range(nblocks):
        term = dot(left6(filtered[b], 0), right6(both[b], 0), (0, 0))
        total = term if total is None else total + term
    width = filtered[0].shape[1]
    correlation, half = total[:, :width], total[:, width:]
    mixed = half + half.T
    rows, cols = iotas((width, width))
    packed = jnp.where(rows >= cols, correlation, mixed)
    diagonal = jnp.sum(jnp.where(rows == cols, mixed, 0.0), axis=0, keepdims=True)
    mid = width // 2

    def put(top_ref, low_ref):
        top_ref[0:mid, :] = packed[:mid]
        top_ref[mid : mid + 8, :] = jnp.broadcast_to(diagonal, (8, width))
        low_ref[0:mid, :] = packed[mid:]
        low_ref[mid : mid + 8, :] = jnp.broadcast_to(diagonal, (8, width))

    @pl.when(parity == 0)
    def _():
        put(keep_ref, send_ref)

    @pl.when(parity != 0)
    def _():
        put(send_ref, keep_ref)


def factor(full, inv_ref, group=8):
    width = full.shape[1]
    tiles = width // 8
    sub, lane = iotas((8, width))
    nought = jnp.where(lane < 0, 1.0, 0.0)

    def along(x, column):
        return jnp.broadcast_to(x[:, column : column + 1], (8, width))

    def down(x, row):
        return jnp.broadcast_to(x[row : row + 1, :], (8, width))

    work = [full[8 * t : 8 * t + 8, :] for t in range(tiles)]
    col, done = [], []
    for p in range(tiles):
        at = 8 * p
        start = p - p % group
        end = min(tiles, start + group)
        inside = (lane >= at) & (lane < at + 8)
        if p == start:
            done = []
            col = [along(work[p], at + j) + nought for j in range(8)]
        raw = {(t, j): along(work[t], at + j) for j in range(8) for t in range(p + 1, end)}
        diagonal, recip, m = [], [], {}
        for j in range(8):
            diagonal.append(down(col[j], j))
            recip.append(1.0 / diagonal[j])
            for k in range(j + 1, 8):
                m[k, j] = down(col[j], k) * recip[j]
                col[k] = col[k] - col[j] * m[k, j]
        coming = []
        if p + 1 < end:
            w = [raw[p + 1, j] + nought for j in range(8)]
            coming = [along(work[p + 1], at + 8 + k) + nought for k in range(8)]
            for j in range(8):
                for k in range(j + 1, 8):
                    w[k] = w[k] - w[j] * m[k, j]
                for k in range(8):
                    coming[k] = coming[k] - w[j] * (down(w[j], k) * recip[j])
        cleared = jnp.where(inside, jnp.where(lane == sub + at, 1.0, 0.0), work[p])
        pivot = []
        for j in range(8):
            r = down(cleared, j)
            for k in range(j):
                r = r - m[j, k] * pivot[k]
            pivot.append(r)
        out = jnp.zeros((8, width), jnp.float32)
        for j in range(8):
            out = jnp.where(sub == j, pivot[j] * lax.rsqrt(diagonal[j]), out)
        inv_ref[at : at + 8, :] = jnp.where(lane <= sub + at, out, 0.0)
        done.append(jnp.where((lane > sub + at) & (lane < 8 * end), 0.0, out))
        solved = [None] * 8
        for k in reversed(range(8)):
            q = pivot[k] * recip[k]
            for j in reversed(range(k + 1, 8)):
                q = q - m[j, k] * solved[j]
            solved[k] = q
        for t in range(p + 1, end):
            acc = jnp.where(inside, 0.0, work[t])
            for j in reversed(range(8)):
                acc = acc - raw[t, j] * solved[j]
            work[t] = acc
        col = coming
        if p + 1 == end < tiles:
            rows = jnp.concatenate(done, 0)
            update = dot(left6(rows, 0), right6(rows, 0), (0, 0))
            for t in range(end, tiles):
                kept = jnp.where((lane >= 8 * start) & (lane < 8 * end), 0.0, work[t])
                work[t] = kept - update[8 * t : 8 * t + 8]


def finish(axis, total_nodes, mine_ref, other_ref, filt_ref, orth_hbm, proj_hbm, inv_ref, orth_ref, proj_ref, sems):
    nblocks, _, width = filt_ref.shape
    mid = width // 2
    swapped = lax.rem(lax.axis_index(axis), 2) != 0
    mine, other = mine_ref[...], other_ref[...]
    top = jnp.where(swapped, other, mine)
    low = jnp.where(swapped, mine, other)
    packed = jnp.concatenate([top[:mid], low[:mid]], 0)
    rows, cols = iotas((width, width))
    turned = packed.T
    full = jnp.where(rows >= cols, packed, turned)
    mixed = jnp.where(rows < cols, packed, jnp.where(rows > cols, turned, top[mid : mid + 1, :]))
    factor(full, inv_ref)
    inv = inv_ref[...]
    inv_r = right6(inv, 1)
    half = dot(left6(inv), right6(mixed))
    grown = right6(inv * math.sqrt(total_nodes), 1)
    copies = []

    def send(source, target):
        copies.append(pltpu.make_async_copy(source, target, sems.at[len(copies)]))
        copies[-1].start()

    for b in range(nblocks):
        orth_ref[b] = dot(left6(filt_ref[b]), grown, (1, 1))
        send(orth_ref.at[b], orth_hbm.at[b])
        if b == 0:
            proj_ref[...] = dot(left6(half), inv_r, (1, 1))
            send(proj_ref, proj_hbm)
    for copy in copies:
        copy.wait()


def shape(*dims, kind=jnp.float32):
    return jax.ShapeDtypeStruct(dims, kind)


def add_up(values, axis, stride=1):
    count = lax.axis_size(axis)
    index = lax.axis_index(axis)
    while stride < count:
        left = count // stride
        radix = 4 if left % 4 == 0 else next(r for r in range(2, left + 1) if left % r == 0)

        def route(partner):
            digits = [(i // stride) % radix for i in range(count)]
            return [(i, i + (partner(k) - k) * stride) for i, k in enumerate(digits)]

        if radix in (2, 4):
            parts = [values]
            for flip in range(1, radix):
                parts.append(lax.ppermute(values, axis, route(lambda k: k ^ flip)))
            while len(parts) > 1:
                parts = [a + b for a, b in zip(parts[::2], parts[1::2])]
            values = parts[0]
        else:
            place = (index // stride) % radix
            parts = [values]
            for hop in range(1, radix):
                parts.append(lax.ppermute(values, axis, route(lambda k: (k - hop) % radix)))
            stacked = jnp.stack(parts)
            total = None
            for digit in range(radix):
                term = lax.dynamic_index_in_dim(stacked, (digit - place) % radix, 0, keepdims=False)
                total = term if total is None else total + term
            values = total
        stride *= radix
    return values


def swap(values, axis, start):
    count = lax.axis_size(axis)
    route = []
    for i in range(start, count - 1 + (start if count % 2 == 0 else 0), 2):
        other = (i + 1) % count
        route += [(i, other), (other, i)]
    return lax.ppermute(values, axis, route)


def body(states, diag_blocks, couplings):
    axis = "dom"
    nodes_dev, width = states.shape
    nblocks, block, _ = diag_blocks.shape
    devices = lax.axis_size(axis)
    field = states.reshape(nblocks, block, width)
    params = pltpu.CompilerParams(vmem_limit_bytes=40 << 20)
    cross = shape(3 * block + block // 2 + 8, width)
    tall = shape(nblocks, block, width)
    square = shape(nblocks, block, block)
    wide = shape(nblocks, block, 3 * block, kind=jnp.bfloat16)

    def call(kernel, ins, outs, scratch=()):
        return pl.pallas_call(
            kernel,
            out_shape=tuple(s for s, spec in outs),
            in_specs=ins,
            out_specs=tuple(spec for s, spec in outs),
            scratch_shapes=scratch,
            compiler_params=params,
        )

    odd, s, d, c = call(
        lambda *refs: edge(axis, *refs),
        [far] * 3,
        [(cross, here), (tall, here), (square, here), (square, here)],
        [pltpu.SemaphoreType.DMA((3,))],
    )(*(pltpu.with_memory_space_constraint(x, pltpu.HBM) for x in (field, diag_blocks, couplings)))
    odd = swap(odd, axis, 1)
    even, sym, cl, ct, first, pre, onward = call(
        lambda *refs: inner(axis, *refs),
        [here] * 3,
        [(cross, here), (wide, here), (wide, here), (wide, here), (tall, here), (tall, here), (shape(block, width), here)],
    )(s, d, c)
    even = swap(even, axis, 0)
    piece = shape(width // 2 + 8, width)
    filtered, keep, send = call(
        lambda *refs: project(axis, *refs), [here] * 9, [(tall, here), (piece, here), (piece, here)]
    )(s, sym, cl, ct, first, pre, onward, even, odd)
    mine = add_up(keep + swap(send, axis, 0), axis, 2)
    other = swap(mine, axis, 0)
    orthonormal, projected = call(
        lambda *refs: finish(axis, nodes_dev * devices, *refs),
        [here] * 3,
        [(tall, far), (shape(width, width), far)],
        [
            pltpu.VMEM((width, width), jnp.float32),
            pltpu.VMEM((nblocks, block, width), jnp.float32),
            pltpu.VMEM((width, width), jnp.float32),
            pltpu.SemaphoreType.DMA((nblocks + 1,)),
        ],
    )(mine, other, filtered)
    return orthonormal.reshape(nodes_dev, width), projected


def solution(mesh):
    in_specs = (P("dom", None), P("dom", None, None), P("dom", None, None))
    out_specs = (P("dom", None), P())

    return jax.shard_map(body, mesh=mesh, in_specs=in_specs, out_specs=out_specs, check_vma=False)
```

```python
import math

import jax
import jax.numpy as jnp
from jax import lax
from jax.experimental import pallas as pl
from jax.experimental.pallas import tpu as pltpu
from jax.sharding import PartitionSpec as P

center = 0.5
half_width = 4.0
scale = 2.0 / half_width
here = pl.BlockSpec(memory_space=pltpu.VMEM)
far = pl.BlockSpec(memory_space=pltpu.HBM)


def two(x):
    high = x.astype(jnp.bfloat16)
    return high, (x - high.astype(jnp.float32)).astype(jnp.bfloat16)


def three(x):
    high = x.astype(jnp.bfloat16)
    rest = x - high.astype(jnp.float32)
    mid = rest.astype(jnp.bfloat16)
    return high, mid, (rest - mid.astype(jnp.float32)).astype(jnp.bfloat16)


def dot(a, b, on=(1, 0)):
    return lax.dot_general(a, b, (((on[0],), (on[1],)), ((), ())), preferred_element_type=jnp.float32)


def left3(x, axis=1):
    high, low = two(x)
    return jnp.concatenate([high, high, low], axis)


def right3(x, axis=0):
    high, low = two(x)
    return jnp.concatenate([high, low, high], axis)


def left6(x, axis=1):
    high, mid, low = three(x)
    return jnp.concatenate([high, high, mid, high, low, mid], axis)


def right6(x, axis=0):
    high, mid, low = three(x)
    return jnp.concatenate([high, mid, high, low, high, mid], axis)


def beside(a, b):
    return jnp.concatenate([a, b], 1)


def stack(a, b):
    return jnp.concatenate([a, b], 0)


def iotas(shape):
    return (
        lax.broadcasted_iota(jnp.int32, shape, 0),
        lax.broadcasted_iota(jnp.int32, shape, 1),
    )


def symmetric(d):
    rows, cols = iotas(d.shape)
    return 0.5 * (d + d.T) - jnp.where(rows == cols, center, 0.0)


def pack(sym):
    block = sym.shape[0]
    mid = block // 2
    rows, cols = iotas((mid, block))
    top, low = sym[:mid], sym[mid:]
    body = jnp.where((cols >= mid) | (rows >= cols), top, pltpu.roll(low, mid, 1))
    diagonal = jnp.sum(jnp.where(cols == rows + mid, low, 0.0), axis=0, keepdims=True)
    return jnp.concatenate([body, jnp.broadcast_to(diagonal, (8, block))], 0)


def unpack(packed):
    block = packed.shape[1]
    mid = block // 2
    rows, cols = iotas((mid, block))
    body, diagonal = packed[:mid], packed[mid : mid + 1]
    top = jnp.where((cols >= mid) | (rows > cols), body, 0.0)
    low = pltpu.roll(jnp.where((cols < mid) & (rows < cols), body, 0.0), mid, 1)
    part = jnp.concatenate([top, low], 0)
    middle = jnp.concatenate([jnp.where(rows == cols, body, 0.0), jnp.where(cols == rows + mid, diagonal, 0.0)], 0)
    return part + part.T + middle


def leftward(s0, s1, s2, sym0, sym1, c0, c1, out_ref, more_ref):
    block = s0.shape[0]
    l0, r0, r1 = left3(sym0), right3(s0), right3(s1)
    c0l = left3(c0)
    part = (dot(l0, r0) + dot(c0l, r1)) / half_width
    first1 = (dot(left3(sym1), r1) + dot(left3(c1), right3(s2)) + dot(left3(c0.T), r0)) / half_width
    out_ref[0:block] = s0
    out_ref[block : 2 * block] = part
    out_ref[2 * block : 2 * block + block // 2 + 8] = pack(sym0)
    more_ref[...] = scale * (dot(l0, right3(part)) + dot(c0l, right3(first1))) - s0


def rightward(s_prev, s_last, sym_last, c_prev, c_last, out_ref, more_ref):
    block = s_last.shape[0]
    rl = right3(s_last)
    part = (dot(left3(sym_last), rl) + dot(left3(c_prev.T), right3(s_prev))) / half_width
    turned = left3(c_last.T)
    out_ref[0:block] = dot(turned, rl)
    out_ref[block : 2 * block] = dot(turned, right3(part))
    out_ref[2 * block : 2 * block + block // 2 + 8] = pack(dot(turned, right3(c_last)))
    more_ref[...] = jnp.zeros_like(c_last)


def edge(axis, s_hbm, d_hbm, c_hbm, odd_ref, s_ref, d_ref, c_ref, sems):
    nblocks = d_hbm.shape[0]
    last = nblocks - 1
    parity = lax.rem(lax.axis_index(axis), 2)
    block = s_hbm.shape[1]
    swap_ref, more_ref = odd_ref.at[: odd_ref.shape[0] - block], odd_ref.at[odd_ref.shape[0] - block :]
    is_last = lax.axis_index(axis) == lax.axis_size(axis) - 1
    copies = []
    for k, (source, target) in enumerate(((s_hbm, s_ref), (d_hbm, d_ref), (c_hbm, c_ref))):
        copies.append(pltpu.make_async_copy(source, target, sems.at[k]))
    for copy in copies:
        copy.start()
    for copy in copies:
        copy.wait()

    @pl.when(is_last)
    def _():
        c_ref[last] = jnp.zeros_like(c_ref[last])

    @pl.when(parity == 0)
    def _():
        leftward(s_ref[0], s_ref[1], s_ref[2], symmetric(d_ref[0]), symmetric(d_ref[1]), c_ref[0], c_ref[1], swap_ref, more_ref)

    @pl.when(parity != 0)
    def _():
        rightward(s_ref[last - 1], s_ref[last], symmetric(d_ref[last]), c_ref[last - 1], c_ref[last], swap_ref, more_ref)


def inner(axis, s_ref, d_ref, c_ref, even_ref, sym_ref, cl_ref, ct_ref, first_ref, pre_ref, pass_ref):
    nblocks = d_ref.shape[0]
    last = nblocks - 1
    block = s_ref.shape[1]
    parity = lax.rem(lax.axis_index(axis), 2)
    swap_ref, more_ref = even_ref.at[: even_ref.shape[0] - block], even_ref.at[even_ref.shape[0] - block :]

    @pl.when(parity != 0)
    def _():
        leftward(s_ref[0], s_ref[1], s_ref[2], symmetric(d_ref[0]), symmetric(d_ref[1]), c_ref[0], c_ref[1], swap_ref, more_ref)

    @pl.when(parity == 0)
    def _():
        rightward(s_ref[last - 1], s_ref[last], symmetric(d_ref[last]), c_ref[last - 1], c_ref[last], swap_ref, more_ref)

    s = [s_ref[b] for b in range(nblocks)]
    sr = [right3(x) for x in s]
    for b in range(nblocks):
        sym_ref[b] = left3(symmetric(d_ref[b]))
        cl_ref[b] = left3(c_ref[b])
        ct_ref[b] = left3(c_ref[b].T)
    first = []
    for b in range(nblocks):
        acc = dot(sym_ref[b], sr[b])
        if b < last:
            acc += dot(cl_ref[b], sr[b + 1])
        if b > 0:
            acc += dot(ct_ref[b - 1], sr[b - 1])
        first.append(acc / half_width)
        first_ref[b] = first[b]
    pass_ref[...] = dot(ct_ref[last], sr[last])
    fr = [right3(x) for x in first]
    for b in range(nblocks):
        acc = None
        terms = []
        if 0 < b < last:
            terms.append((sym_ref, b, b))
        if b + 1 < last:
            terms.append((cl_ref, b, b + 1))
        if b > 1:
            terms.append((ct_ref, b - 1, b - 1))
        for ref, which, operand in terms:
            term = dot(ref[which], fr[operand])
            acc = term if acc is None else acc + term
        pre_ref[b] = -s[b] if acc is None else scale * acc - s[b]


def project(axis, s_ref, sym_ref, cl_ref, ct_ref, first_ref, pre_ref, pass_ref, even_ref, odd_ref, filt_ref, keep_ref, send_ref):
    nblocks, block, unused = s_ref.shape
    last = nblocks - 1
    parity = lax.rem(lax.axis_index(axis), 2)
    rows = odd_ref.shape[0] - block
    cuts = ((0, block), (block, 2 * block), (2 * block, rows))
    right = [jnp.where(parity == 0, even_ref[a:b], odd_ref[a:b]) for a, b in cuts]
    left = [jnp.where(parity == 0, odd_ref[a:b], even_ref[a:b]) for a, b in cuts]
    other = jnp.where(parity == 0, even_ref[rows:], odd_ref[rows:])
    onward = pass_ref[...]
    tail = first_ref[last] + dot(cl_ref[last], right3(right[0])) / half_width
    head = first_ref[0] + left[0] / half_width
    ahead = right[1] + onward / half_width
    behind = left[1] + dot(left3(unpack(left[2])), right3(s_ref[0])) / half_width
    tail_r, head_r = right3(tail), right3(head)
    filtered = [pre_ref[b] for b in range(nblocks)]
    filtered[0] += scale * (dot(sym_ref[0], head_r) + behind)
    filtered[1] += scale * dot(ct_ref[0], head_r)
    filtered[last - 1] += scale * dot(cl_ref[last - 1], tail_r)
    filtered[last] += scale * dot(beside(sym_ref[last], cl_ref[last]), stack(tail_r, right3(ahead)))
    beyond = other + scale * (dot(left3(unpack(right[2])), right3(onward)) / half_width + dot(ct_ref[last], tail_r))
    filtered.append(beyond)
    fr = [right3(x) for x in filtered]
    images = []
    for b in range(nblocks):
        filt_ref[b] = filtered[b]
        image = dot(beside(sym_ref[b] * 0.5, cl_ref[b]), stack(fr[b], fr[b + 1])) + 0.5 * center * filtered[b]
        images.append(image)
    total, fine = None, None
    for b in range(nblocks):
        (high, mid, low), (ihigh, imid, unused) = three(filtered[b]), three(images[b])
        upper = jnp.concatenate([jnp.concatenate([high, mid, high], 0), jnp.concatenate([ihigh, imid, ihigh], 0)], 1)
        term = dot(jnp.concatenate([high, high, mid], 0), upper, (0, 0))
        extra = dot(jnp.concatenate([high, low, mid], 0), jnp.concatenate([low, high, mid], 0), (0, 0))
        total = term if total is None else total + term
        fine = extra if fine is None else fine + extra
    width = filtered[0].shape[1]
    correlation, half = total[:, :width] + fine, total[:, width:]
    mixed = half + half.T
    rows, cols = iotas((width, width))
    packed = jnp.where(rows >= cols, correlation, mixed)
    diagonal = jnp.sum(jnp.where(rows == cols, mixed, 0.0), axis=0, keepdims=True)
    mid = width // 2

    def put(top_ref, low_ref):
        top_ref[0:mid, :] = packed[:mid]
        top_ref[mid : mid + 8, :] = jnp.broadcast_to(diagonal, (8, width))
        low_ref[0:mid, :] = packed[mid:]
        low_ref[mid : mid + 8, :] = jnp.broadcast_to(diagonal, (8, width))

    @pl.when(parity == 0)
    def _():
        put(keep_ref, send_ref)

    @pl.when(parity != 0)
    def _():
        put(send_ref, keep_ref)


def factor(full, inv_ref, group=8):
    width = full.shape[1]
    tiles = width // 8
    sub, lane = iotas((8, width))
    nought = jnp.where(lane < 0, 1.0, 0.0)

    def along(x, column):
        return jnp.broadcast_to(x[:, column : column + 1], (8, width))

    def down(x, row):
        return jnp.broadcast_to(x[row : row + 1, :], (8, width))

    work = [full[8 * t : 8 * t + 8, :] for t in range(tiles)]
    col, done = [], []
    for p in range(tiles):
        at = 8 * p
        start = p - p % group
        end = min(tiles, start + group)
        inside = (lane >= at) & (lane < at + 8)
        if p == start:
            done = []
            col = [along(work[p], at + j) + nought for j in range(8)]
        raw = {(t, j): along(work[t], at + j) for j in range(8) for t in range(p + 1, end)}
        diagonal, recip, m = [], [], {}
        for j in range(8):
            diagonal.append(down(col[j], j))
            recip.append(1.0 / diagonal[j])
            for k in range(j + 1, 8):
                m[k, j] = down(col[j], k) * recip[j]
                col[k] = col[k] - col[j] * m[k, j]
        coming = []
        if p + 1 < end:
            w = [raw[p + 1, j] + nought for j in range(8)]
            coming = [along(work[p + 1], at + 8 + k) + nought for k in range(8)]
            for j in range(8):
                for k in range(j + 1, 8):
                    w[k] = w[k] - w[j] * m[k, j]
                for k in range(8):
                    coming[k] = coming[k] - w[j] * (down(w[j], k) * recip[j])
        cleared = jnp.where(inside, jnp.where(lane == sub + at, 1.0, 0.0), work[p])
        pivot = []
        for j in range(8):
            r = down(cleared, j)
            for k in range(j):
                r = r - m[j, k] * pivot[k]
            pivot.append(r)
        out = jnp.zeros((8, width), jnp.float32)
        for j in range(8):
            out = jnp.where(sub == j, pivot[j] * lax.rsqrt(diagonal[j]), out)
        inv_ref[at : at + 8, :] = jnp.where(lane <= sub + at, out, 0.0)
        done.append(jnp.where((lane > sub + at) & (lane < 8 * end), 0.0, out))
        solved = [None] * 8
        for k in reversed(range(8)):
            q = pivot[k] * recip[k]
            for j in reversed(range(k + 1, 8)):
                q = q - m[j, k] * solved[j]
            solved[k] = q
        for t in range(p + 1, end):
            acc = jnp.where(inside, 0.0, work[t])
            for j in reversed(range(8)):
                acc = acc - raw[t, j] * solved[j]
            work[t] = acc
        col = coming
        if p + 1 == end < tiles:
            rows = jnp.concatenate(done, 0)
            update = dot(left6(rows, 0), right6(rows, 0), (0, 0))
            for t in range(end, tiles):
                kept = jnp.where((lane >= 8 * start) & (lane < 8 * end), 0.0, work[t])
                work[t] = kept - update[8 * t : 8 * t + 8]


def finish(axis, total_nodes, mine_ref, other_ref, filt_ref, orth_hbm, proj_hbm, inv_ref, orth_ref, proj_ref, sems):
    nblocks, _, width = filt_ref.shape
    mid = width // 2
    swapped = lax.rem(lax.axis_index(axis), 2) != 0
    mine, other = mine_ref[...], other_ref[...]
    top = jnp.where(swapped, other, mine)
    low = jnp.where(swapped, mine, other)
    packed = jnp.concatenate([top[:mid], low[:mid]], 0)
    rows, cols = iotas((width, width))
    turned = packed.T
    full = jnp.where(rows >= cols, packed, turned)
    mixed = jnp.where(rows < cols, packed, jnp.where(rows > cols, turned, top[mid : mid + 1, :]))
    factor(full, inv_ref)
    inv = inv_ref[...]
    inv_r = right6(inv, 1)
    half = dot(left6(inv), right6(mixed))
    grown = right6(inv * math.sqrt(total_nodes), 1)
    copies = []

    def send(source, target):
        copies.append(pltpu.make_async_copy(source, target, sems.at[len(copies)]))
        copies[-1].start()

    for b in range(nblocks):
        orth_ref[b] = dot(left6(filt_ref[b]), grown, (1, 1))
        send(orth_ref.at[b], orth_hbm.at[b])
        if b == 0:
            proj_ref[...] = dot(left6(half), inv_r, (1, 1))
            send(proj_ref, proj_hbm)
    for copy in copies:
        copy.wait()


def shape(*dims, kind=jnp.float32):
    return jax.ShapeDtypeStruct(dims, kind)


def add_up(values, axis, stride=1):
    count = lax.axis_size(axis)
    index = lax.axis_index(axis)
    while stride < count:
        left = count // stride
        radix = 4 if left % 4 == 0 else next(r for r in range(2, left + 1) if left % r == 0)

        def route(partner):
            digits = [(i // stride) % radix for i in range(count)]
            return [(i, i + (partner(k) - k) * stride) for i, k in enumerate(digits)]

        if radix in (2, 4):
            parts = [values]
            for flip in range(1, radix):
                parts.append(lax.ppermute(values, axis, route(lambda k: k ^ flip)))
            while len(parts) > 1:
                parts = [a + b for a, b in zip(parts[::2], parts[1::2])]
            values = parts[0]
        else:
            place = (index // stride) % radix
            parts = [values]
            for hop in range(1, radix):
                parts.append(lax.ppermute(values, axis, route(lambda k: (k - hop) % radix)))
            stacked = jnp.stack(parts)
            total = None
            for digit in range(radix):
                term = lax.dynamic_index_in_dim(stacked, (digit - place) % radix, 0, keepdims=False)
                total = term if total is None else total + term
            values = total
        stride *= radix
    return values


def swap(values, axis, start):
    count = lax.axis_size(axis)
    route = []
    for i in range(start, count - 1 + (start if count % 2 == 0 else 0), 2):
        other = (i + 1) % count
        route += [(i, other), (other, i)]
    return lax.ppermute(values, axis, route)


def body(states, diag_blocks, couplings):
    axis = "dom"
    nodes_dev, width = states.shape
    nblocks, block, _ = diag_blocks.shape
    devices = lax.axis_size(axis)
    field = states.reshape(nblocks, block, width)
    params = pltpu.CompilerParams(vmem_limit_bytes=40 << 20)
    cross = shape(3 * block + block // 2 + 8, width)
    tall = shape(nblocks, block, width)
    square = shape(nblocks, block, block)
    wide = shape(nblocks, block, 3 * block, kind=jnp.bfloat16)

    def call(kernel, ins, outs, scratch=()):
        return pl.pallas_call(
            kernel,
            out_shape=tuple(s for s, spec in outs),
            in_specs=ins,
            out_specs=tuple(spec for s, spec in outs),
            scratch_shapes=scratch,
            compiler_params=params,
        )

    odd, s, d, c = call(
        lambda *refs: edge(axis, *refs),
        [far] * 3,
        [(cross, here), (tall, here), (square, here), (square, here)],
        [pltpu.SemaphoreType.DMA((3,))],
    )(*(pltpu.with_memory_space_constraint(x, pltpu.HBM) for x in (field, diag_blocks, couplings)))
    odd = swap(odd, axis, 1)
    even, sym, cl, ct, first, pre, onward = call(
        lambda *refs: inner(axis, *refs),
        [here] * 3,
        [(cross, here), (wide, here), (wide, here), (wide, here), (tall, here), (tall, here), (shape(block, width), here)],
    )(s, d, c)
    even = swap(even, axis, 0)
    piece = shape(width // 2 + 8, width)
    filtered, keep, send = call(
        lambda *refs: project(axis, *refs), [here] * 9, [(tall, here), (piece, here), (piece, here)]
    )(s, sym, cl, ct, first, pre, onward, even, odd)
    mine = add_up(keep + swap(send, axis, 0), axis, 2)
    other = swap(mine, axis, 0)
    orthonormal, projected = call(
        lambda *refs: finish(axis, nodes_dev * devices, *refs),
        [here] * 3,
        [(tall, far), (shape(width, width), far)],
        [
            pltpu.VMEM((width, width), jnp.float32),
            pltpu.VMEM((nblocks, block, width), jnp.float32),
            pltpu.VMEM((width, width), jnp.float32),
            pltpu.SemaphoreType.DMA((nblocks + 1,)),
        ],
    )(mine, other, filtered)
    return orthonormal.reshape(nodes_dev, width), projected


def solution(mesh):
    in_specs = (P("dom", None), P("dom", None, None), P("dom", None, None))
    out_specs = (P("dom", None), P())

    return jax.shard_map(body, mesh=mesh, in_specs=in_specs, out_specs=out_specs, check_vma=False)
```

```python
import math

import jax
import jax.numpy as jnp
from jax import lax
from jax.experimental import pallas as pl
from jax.experimental.pallas import tpu as pltpu
from jax.sharding import PartitionSpec as P

center = 0.5
half_width = 4.0
scale = 2.0 / half_width
here = pl.BlockSpec(memory_space=pltpu.VMEM)
far = pl.BlockSpec(memory_space=pltpu.HBM)


def two(x):
    high = x.astype(jnp.bfloat16)
    return high, (x - high.astype(jnp.float32)).astype(jnp.bfloat16)


def three(x):
    high = x.astype(jnp.bfloat16)
    rest = x - high.astype(jnp.float32)
    mid = rest.astype(jnp.bfloat16)
    return high, mid, (rest - mid.astype(jnp.float32)).astype(jnp.bfloat16)


def dot(a, b, on=(1, 0)):
    return lax.dot_general(a, b, (((on[0],), (on[1],)), ((), ())), preferred_element_type=jnp.float32)


def left3(x, axis=1):
    high, low = two(x)
    return jnp.concatenate([high, high, low], axis)


def right3(x, axis=0):
    high, low = two(x)
    return jnp.concatenate([high, low, high], axis)


def left6(x, axis=1):
    high, mid, low = three(x)
    return jnp.concatenate([high, high, mid, high, low, mid], axis)


def right6(x, axis=0):
    high, mid, low = three(x)
    return jnp.concatenate([high, mid, high, low, high, mid], axis)


def beside(a, b):
    return jnp.concatenate([a, b], 1)


def stack(a, b):
    return jnp.concatenate([a, b], 0)


def iotas(shape):
    return (
        lax.broadcasted_iota(jnp.int32, shape, 0),
        lax.broadcasted_iota(jnp.int32, shape, 1),
    )


def symmetric(d):
    rows, cols = iotas(d.shape)
    return 0.5 * (d + d.T) - jnp.where(rows == cols, center, 0.0)


def pack(sym):
    block = sym.shape[0]
    mid = block // 2
    rows, cols = iotas((mid, block))
    top, low = sym[:mid], sym[mid:]
    body = jnp.where((cols >= mid) | (rows >= cols), top, pltpu.roll(low, mid, 1))
    diagonal = jnp.sum(jnp.where(cols == rows + mid, low, 0.0), axis=0, keepdims=True)
    return jnp.concatenate([body, jnp.broadcast_to(diagonal, (8, block))], 0)


def unpack(packed):
    block = packed.shape[1]
    mid = block // 2
    rows, cols = iotas((mid, block))
    body, diagonal = packed[:mid], packed[mid : mid + 1]
    top = jnp.where((cols >= mid) | (rows > cols), body, 0.0)
    low = pltpu.roll(jnp.where((cols < mid) & (rows < cols), body, 0.0), mid, 1)
    part = jnp.concatenate([top, low], 0)
    middle = jnp.concatenate([jnp.where(rows == cols, body, 0.0), jnp.where(cols == rows + mid, diagonal, 0.0)], 0)
    return part + part.T + middle


def leftward(s0, s1, s2, sym0, sym1, c0, c1, out_ref, more_ref):
    block = s0.shape[0]
    l0, r0, r1 = left3(sym0), right3(s0), right3(s1)
    c0l = left3(c0)
    part = (dot(l0, r0) + dot(c0l, r1)) / half_width
    first1 = (dot(left3(sym1), r1) + dot(left3(c1), right3(s2)) + dot(left3(c0.T), r0)) / half_width
    out_ref[0:block] = s0
    out_ref[block : 2 * block] = part
    out_ref[2 * block : 2 * block + block // 2 + 8] = pack(sym0)
    more_ref[...] = scale * (dot(l0, right3(part)) + dot(c0l, right3(first1))) - s0


def rightward(s_prev, s_last, sym_last, c_prev, c_last, out_ref, more_ref):
    block = s_last.shape[0]
    rl = right3(s_last)
    part = (dot(left3(sym_last), rl) + dot(left3(c_prev.T), right3(s_prev))) / half_width
    turned = left3(c_last.T)
    out_ref[0:block] = dot(turned, rl)
    out_ref[block : 2 * block] = dot(turned, right3(part))
    out_ref[2 * block : 2 * block + block // 2 + 8] = pack(dot(turned, right3(c_last)))
    more_ref[...] = jnp.zeros_like(c_last)


def load(pairs, sems):
    copies = [pltpu.make_async_copy(source, target, sems.at[k]) for k, (source, target) in enumerate(pairs)]
    for copy in copies:
        copy.start()
    for copy in copies:
        copy.wait()


def cut(axis, c_ref, last):
    @pl.when(lax.axis_index(axis) == lax.axis_size(axis) - 1)
    def _():
        c_ref[last] = jnp.zeros_like(c_ref[last])


def edge(axis, s_hbm, d_hbm, c_hbm, odd_ref, s_ref, d_ref, c_ref, sems):
    nblocks, block, _ = d_hbm.shape
    last = nblocks - 1
    parity = lax.rem(lax.axis_index(axis), 2)
    swap_ref, more_ref = odd_ref.at[: odd_ref.shape[0] - block], odd_ref.at[odd_ref.shape[0] - block :]

    def bring(s_range, d_range, c_range):
        ranges = ((s_hbm, s_ref, s_range), (d_hbm, d_ref, d_range), (c_hbm, c_ref, c_range))
        load([(x.at[a:b], y.at[a:b]) for x, y, (a, b) in ranges], sems)

    @pl.when(parity == 0)
    def _():
        bring((0, 3), (0, 2), (0, 2))
        leftward(s_ref[0], s_ref[1], s_ref[2], symmetric(d_ref[0]), symmetric(d_ref[1]), c_ref[0], c_ref[1], swap_ref, more_ref)

    @pl.when(parity != 0)
    def _():
        bring((last - 1, nblocks), (last, nblocks), (last - 1, nblocks))
        cut(axis, c_ref, last)
        rightward(s_ref[last - 1], s_ref[last], symmetric(d_ref[last]), c_ref[last - 1], c_ref[last], swap_ref, more_ref)


def inner(axis, s_hbm, d_hbm, c_hbm, s_ref, even_ref, sym_ref, cl_ref, ct_ref, first_ref, pre_ref, pass_ref, d_ref, c_ref, sems):
    nblocks, block, _ = d_hbm.shape
    last = nblocks - 1
    parity = lax.rem(lax.axis_index(axis), 2)
    swap_ref, more_ref = even_ref.at[: even_ref.shape[0] - block], even_ref.at[even_ref.shape[0] - block :]
    load(((s_hbm, s_ref), (d_hbm, d_ref), (c_hbm, c_ref)), sems)
    cut(axis, c_ref, last)

    @pl.when(parity != 0)
    def _():
        leftward(s_ref[0], s_ref[1], s_ref[2], symmetric(d_ref[0]), symmetric(d_ref[1]), c_ref[0], c_ref[1], swap_ref, more_ref)

    @pl.when(parity == 0)
    def _():
        rightward(s_ref[last - 1], s_ref[last], symmetric(d_ref[last]), c_ref[last - 1], c_ref[last], swap_ref, more_ref)

    s = [s_ref[b] for b in range(nblocks)]
    sr = [right3(x) for x in s]
    for b in range(nblocks):
        sym_ref[b] = left3(symmetric(d_ref[b]))
        cl_ref[b] = left3(c_ref[b])
        ct_ref[b] = left3(c_ref[b].T)
    first = []
    for b in range(nblocks):
        acc = dot(sym_ref[b], sr[b])
        if b < last:
            acc += dot(cl_ref[b], sr[b + 1])
        if b > 0:
            acc += dot(ct_ref[b - 1], sr[b - 1])
        first.append(acc / half_width)
        first_ref[b] = first[b]
    pass_ref[...] = dot(ct_ref[last], sr[last])
    fr = [right3(x) for x in first]
    for b in range(nblocks):
        acc = None
        terms = []
        if 0 < b < last:
            terms.append((sym_ref, b, b))
        if b + 1 < last:
            terms.append((cl_ref, b, b + 1))
        if b > 1:
            terms.append((ct_ref, b - 1, b - 1))
        for ref, which, operand in terms:
            term = dot(ref[which], fr[operand])
            acc = term if acc is None else acc + term
        pre_ref[b] = -s[b] if acc is None else scale * acc - s[b]


def project(axis, s_ref, sym_ref, cl_ref, ct_ref, first_ref, pre_ref, pass_ref, even_ref, odd_ref, filt_ref, keep_ref, send_ref):
    nblocks, block, unused = s_ref.shape
    last = nblocks - 1
    parity = lax.rem(lax.axis_index(axis), 2)
    rows = odd_ref.shape[0] - block
    cuts = ((0, block), (block, 2 * block), (2 * block, rows))
    right = [jnp.where(parity == 0, even_ref[a:b], odd_ref[a:b]) for a, b in cuts]
    left = [jnp.where(parity == 0, odd_ref[a:b], even_ref[a:b]) for a, b in cuts]
    other = jnp.where(parity == 0, even_ref[rows:], odd_ref[rows:])
    onward = pass_ref[...]
    tail = first_ref[last] + dot(cl_ref[last], right3(right[0])) / half_width
    head = first_ref[0] + left[0] / half_width
    ahead = right[1] + onward / half_width
    behind = left[1] + dot(left3(unpack(left[2])), right3(s_ref[0])) / half_width
    tail_r, head_r = right3(tail), right3(head)
    filtered = [pre_ref[b] for b in range(nblocks)]
    filtered[0] += scale * (dot(sym_ref[0], head_r) + behind)
    filtered[1] += scale * dot(ct_ref[0], head_r)
    filtered[last - 1] += scale * dot(cl_ref[last - 1], tail_r)
    filtered[last] += scale * dot(beside(sym_ref[last], cl_ref[last]), stack(tail_r, right3(ahead)))
    beyond = other + scale * (dot(left3(unpack(right[2])), right3(onward)) / half_width + dot(ct_ref[last], tail_r))
    filtered.append(beyond)
    fr = [right3(x) for x in filtered]
    images = []
    for b in range(nblocks):
        filt_ref[b] = filtered[b]
        image = dot(beside(sym_ref[b] * 0.5, cl_ref[b]), stack(fr[b], fr[b + 1])) + 0.5 * center * filtered[b]
        images.append(image)
    total, fine = None, None
    for b in range(nblocks):
        (high, mid, low), (ihigh, imid, unused) = three(filtered[b]), three(images[b])
        upper = jnp.concatenate([jnp.concatenate([high, mid, high], 0), jnp.concatenate([ihigh, imid, ihigh], 0)], 1)
        term = dot(jnp.concatenate([high, high, mid], 0), upper, (0, 0))
        extra = dot(jnp.concatenate([high, low, mid], 0), jnp.concatenate([low, high, mid], 0), (0, 0))
        total = term if total is None else total + term
        fine = extra if fine is None else fine + extra
    width = filtered[0].shape[1]
    correlation, half = total[:, :width] + fine, total[:, width:]
    mixed = half + half.T
    rows, cols = iotas((width, width))
    packed = jnp.where(rows >= cols, correlation, mixed)
    diagonal = jnp.sum(jnp.where(rows == cols, mixed, 0.0), axis=0, keepdims=True)
    mid = width // 2

    def put(top_ref, low_ref):
        top_ref[0:mid, :] = packed[:mid]
        top_ref[mid : mid + 8, :] = jnp.broadcast_to(diagonal, (8, width))
        low_ref[0:mid, :] = packed[mid:]
        low_ref[mid : mid + 8, :] = jnp.broadcast_to(diagonal, (8, width))

    @pl.when(parity == 0)
    def _():
        put(keep_ref, send_ref)

    @pl.when(parity != 0)
    def _():
        put(send_ref, keep_ref)


def factor(full, inv_ref, group=8):
    width = full.shape[1]
    tiles = width // 8
    sub, lane = iotas((8, width))
    nought = jnp.where(lane < 0, 1.0, 0.0)

    def along(x, column):
        return jnp.broadcast_to(x[:, column : column + 1], (8, width))

    def down(x, row):
        return jnp.broadcast_to(x[row : row + 1, :], (8, width))

    work = [full[8 * t : 8 * t + 8, :] for t in range(tiles)]
    col, done = [], []
    for p in range(tiles):
        at = 8 * p
        start = p - p % group
        end = min(tiles, start + group)
        inside = (lane >= at) & (lane < at + 8)
        if p == start:
            done = []
            col = [along(work[p], at + j) + nought for j in range(8)]
        raw = {(t, j): along(work[t], at + j) for j in range(8) for t in range(p + 1, end)}
        diagonal, recip, m = [], [], {}
        for j in range(8):
            diagonal.append(down(col[j], j))
            recip.append(1.0 / diagonal[j])
            for k in range(j + 1, 8):
                m[k, j] = down(col[j], k) * recip[j]
                col[k] = col[k] - col[j] * m[k, j]
        coming = []
        if p + 1 < end:
            w = [raw[p + 1, j] + nought for j in range(8)]
            coming = [along(work[p + 1], at + 8 + k) + nought for k in range(8)]
            for j in range(8):
                for k in range(j + 1, 8):
                    w[k] = w[k] - w[j] * m[k, j]
                for k in range(8):
                    coming[k] = coming[k] - w[j] * (down(w[j], k) * recip[j])
        cleared = jnp.where(inside, jnp.where(lane == sub + at, 1.0, 0.0), work[p])
        pivot = []
        for j in range(8):
            r = down(cleared, j)
            for k in range(j):
                r = r - m[j, k] * pivot[k]
            pivot.append(r)
        out = jnp.zeros((8, width), jnp.float32)
        for j in range(8):
            out = jnp.where(sub == j, pivot[j] * lax.rsqrt(diagonal[j]), out)
        inv_ref[at : at + 8, :] = jnp.where(lane <= sub + at, out, 0.0)
        done.append(jnp.where((lane > sub + at) & (lane < 8 * end), 0.0, out))
        solved = [None] * 8
        for k in reversed(range(8)):
            q = pivot[k] * recip[k]
            for j in reversed(range(k + 1, 8)):
                q = q - m[j, k] * solved[j]
            solved[k] = q
        for t in range(p + 1, end):
            acc = jnp.where(inside, 0.0, work[t])
            for j in reversed(range(8)):
                acc = acc - raw[t, j] * solved[j]
            work[t] = acc
        col = coming
        if p + 1 == end < tiles:
            rows = jnp.concatenate(done, 0)
            update = dot(left6(rows, 0), right6(rows, 0), (0, 0))
            for t in range(end, tiles):
                kept = jnp.where((lane >= 8 * start) & (lane < 8 * end), 0.0, work[t])
                work[t] = kept - update[8 * t : 8 * t + 8]


def finish(axis, total_nodes, mine_ref, other_ref, filt_ref, orth_hbm, proj_hbm, inv_ref, orth_ref, proj_ref, sems):
    nblocks, _, width = filt_ref.shape
    mid = width // 2
    swapped = lax.rem(lax.axis_index(axis), 2) != 0
    mine, other = mine_ref[...], other_ref[...]
    top = jnp.where(swapped, other, mine)
    low = jnp.where(swapped, mine, other)
    packed = jnp.concatenate([top[:mid], low[:mid]], 0)
    rows, cols = iotas((width, width))
    turned = packed.T
    full = jnp.where(rows >= cols, packed, turned)
    mixed = jnp.where(rows < cols, packed, jnp.where(rows > cols, turned, top[mid : mid + 1, :]))
    factor(full, inv_ref)
    inv = inv_ref[...]
    inv_r = right6(inv, 1)
    half = dot(left6(inv), right6(mixed))
    grown = right6(inv * math.sqrt(total_nodes), 1)
    copies = []

    def send(source, target):
        copies.append(pltpu.make_async_copy(source, target, sems.at[len(copies)]))
        copies[-1].start()

    for b in range(nblocks):
        orth_ref[b] = dot(left6(filt_ref[b]), grown, (1, 1))
        send(orth_ref.at[b], orth_hbm.at[b])
        if b == 0:
            proj_ref[...] = dot(left6(half), inv_r, (1, 1))
            send(proj_ref, proj_hbm)
    for copy in copies:
        copy.wait()


def shape(*dims, kind=jnp.float32):
    return jax.ShapeDtypeStruct(dims, kind)


def add_up(values, axis, stride=1):
    count = lax.axis_size(axis)
    index = lax.axis_index(axis)
    while stride < count:
        left = count // stride
        radix = 4 if left % 4 == 0 else next(r for r in range(2, left + 1) if left % r == 0)

        def route(partner):
            digits = [(i // stride) % radix for i in range(count)]
            return [(i, i + (partner(k) - k) * stride) for i, k in enumerate(digits)]

        if radix in (2, 4):
            parts = [values]
            for flip in range(1, radix):
                parts.append(lax.ppermute(values, axis, route((lambda k: (k - flip) % 4) if radix == 4 and stride > 2 else (lambda k: k ^ flip))))
            if radix == 4:
                parts = [parts[0], parts[2], parts[1], parts[3]]
            while len(parts) > 1:
                parts = [a + b for a, b in zip(parts[::2], parts[1::2])]
            values = parts[0]
        else:
            place = (index // stride) % radix
            parts = [values]
            for hop in range(1, radix):
                parts.append(lax.ppermute(values, axis, route(lambda k: (k - hop) % radix)))
            stacked = jnp.stack(parts)
            total = None
            for digit in range(radix):
                term = lax.dynamic_index_in_dim(stacked, (digit - place) % radix, 0, keepdims=False)
                total = term if total is None else total + term
            values = total
        stride *= radix
    return values


def swap(values, axis, start):
    count = lax.axis_size(axis)
    route = []
    for i in range(start, count - 1 + (start if count % 2 == 0 else 0), 2):
        other = (i + 1) % count
        route += [(i, other), (other, i)]
    return lax.ppermute(values, axis, route)


def body(states, diag_blocks, couplings):
    axis = "dom"
    nodes_dev, width = states.shape
    nblocks, block, _ = diag_blocks.shape
    devices = lax.axis_size(axis)
    field = states.reshape(nblocks, block, width)
    params = pltpu.CompilerParams(vmem_limit_bytes=40 << 20)
    cross = shape(3 * block + block // 2 + 8, width)
    tall = shape(nblocks, block, width)
    square = shape(nblocks, block, block)
    wide = shape(nblocks, block, 3 * block, kind=jnp.bfloat16)

    def call(kernel, ins, outs, scratch=()):
        return pl.pallas_call(
            kernel,
            out_shape=tuple(s for s, spec in outs),
            in_specs=ins,
            out_specs=tuple(spec for s, spec in outs),
            scratch_shapes=scratch,
            compiler_params=params,
        )

    inputs = tuple(pltpu.with_memory_space_constraint(x, pltpu.HBM) for x in (field, diag_blocks, couplings))
    squares = [pltpu.VMEM(square.shape, jnp.float32)] * 2 + [pltpu.SemaphoreType.DMA((3,))]
    (odd,) = call(
        lambda *refs: edge(axis, *refs), [far] * 3, [(cross, here)], [pltpu.VMEM(tall.shape, jnp.float32)] + squares
    )(*inputs)
    odd = swap(odd, axis, 1)
    s, even, sym, cl, ct, first, pre, onward = call(
        lambda *refs: inner(axis, *refs),
        [far] * 3,
        [(tall, here), (cross, here), (wide, here), (wide, here), (wide, here), (tall, here), (tall, here), (shape(block, width), here)],
        squares,
    )(*inputs)
    even = swap(even, axis, 0)
    piece = shape(width // 2 + 8, width)
    filtered, keep, send = call(
        lambda *refs: project(axis, *refs), [here] * 9, [(tall, here), (piece, here), (piece, here)]
    )(s, sym, cl, ct, first, pre, onward, even, odd)
    mine = add_up(keep + swap(send, axis, 0), axis, 2)
    other = swap(mine, axis, 0)
    orthonormal, projected = call(
        lambda *refs: finish(axis, nodes_dev * devices, *refs),
        [here] * 3,
        [(tall, far), (shape(width, width), far)],
        [
            pltpu.VMEM((width, width), jnp.float32),
            pltpu.VMEM((nblocks, block, width), jnp.float32),
            pltpu.VMEM((width, width), jnp.float32),
            pltpu.SemaphoreType.DMA((nblocks + 1,)),
        ],
    )(mine, other, filtered)
    return orthonormal.reshape(nodes_dev, width), projected


def solution(mesh):
    in_specs = (P("dom", None), P("dom", None, None), P("dom", None, None))
    out_specs = (P("dom", None), P())

    return jax.shard_map(body, mesh=mesh, in_specs=in_specs, out_specs=out_specs, check_vma=False)
```

```python
import math

import jax
import jax.numpy as jnp
from jax import lax
from jax.experimental import pallas as pl
from jax.experimental.pallas import tpu as pltpu
from jax.sharding import PartitionSpec as P

center = 0.5
half_width = 4.0
scale = 2.0 / half_width
here = pl.BlockSpec(memory_space=pltpu.VMEM)
far = pl.BlockSpec(memory_space=pltpu.HBM)


def two(x):
    high = x.astype(jnp.bfloat16)
    return high, (x - high.astype(jnp.float32)).astype(jnp.bfloat16)


def three(x):
    high = x.astype(jnp.bfloat16)
    rest = x - high.astype(jnp.float32)
    mid = rest.astype(jnp.bfloat16)
    return high, mid, (rest - mid.astype(jnp.float32)).astype(jnp.bfloat16)


def dot(a, b, on=(1, 0)):
    return lax.dot_general(a, b, (((on[0],), (on[1],)), ((), ())), preferred_element_type=jnp.float32)


def left3(x, axis=1):
    high, low = two(x)
    return jnp.concatenate([high, high, low], axis)


def right3(x, axis=0):
    high, low = two(x)
    return jnp.concatenate([high, low, high], axis)


def left6(x, axis=1):
    high, mid, low = three(x)
    return jnp.concatenate([high, high, mid, high, low, mid], axis)


def right6(x, axis=0):
    high, mid, low = three(x)
    return jnp.concatenate([high, mid, high, low, high, mid], axis)


def beside(a, b):
    return jnp.concatenate([a, b], 1)


def stack(a, b):
    return jnp.concatenate([a, b], 0)


def iotas(shape):
    return (
        lax.broadcasted_iota(jnp.int32, shape, 0),
        lax.broadcasted_iota(jnp.int32, shape, 1),
    )


def symmetric(d):
    rows, cols = iotas(d.shape)
    return 0.5 * (d + d.T) - jnp.where(rows == cols, center, 0.0)


def pack(sym):
    block = sym.shape[0]
    mid = block // 2
    rows, cols = iotas((mid, block))
    top, low = sym[:mid], sym[mid:]
    body = jnp.where((cols >= mid) | (rows >= cols), top, pltpu.roll(low, mid, 1))
    diagonal = jnp.sum(jnp.where(cols == rows + mid, low, 0.0), axis=0, keepdims=True)
    return jnp.concatenate([body, jnp.broadcast_to(diagonal, (8, block))], 0)


def unpack(packed):
    block = packed.shape[1]
    mid = block // 2
    rows, cols = iotas((mid, block))
    body, diagonal = packed[:mid], packed[mid : mid + 1]
    top = jnp.where((cols >= mid) | (rows > cols), body, 0.0)
    low = pltpu.roll(jnp.where((cols < mid) & (rows < cols), body, 0.0), mid, 1)
    part = jnp.concatenate([top, low], 0)
    middle = jnp.concatenate([jnp.where(rows == cols, body, 0.0), jnp.where(cols == rows + mid, diagonal, 0.0)], 0)
    return part + part.T + middle


def leftward(s0, s1, s2, sym0, sym1, c0, c1, out_ref, more_ref):
    block = s0.shape[0]
    l0, r0, r1 = left3(sym0), right3(s0), right3(s1)
    c0l = left3(c0)
    part = (dot(l0, r0) + dot(c0l, r1)) / half_width
    first1 = (dot(left3(sym1), r1) + dot(left3(c1), right3(s2)) + dot(left3(c0.T), r0)) / half_width
    out_ref[0:block] = s0
    out_ref[block : 2 * block] = part
    out_ref[2 * block : 2 * block + block // 2 + 8] = pack(sym0)
    more_ref[...] = scale * (dot(l0, right3(part)) + dot(c0l, right3(first1))) - s0


def rightward(s_prev, s_last, sym_last, c_prev, c_last, out_ref, more_ref):
    block = s_last.shape[0]
    rl = right3(s_last)
    part = (dot(left3(sym_last), rl) + dot(left3(c_prev.T), right3(s_prev))) / half_width
    turned = left3(c_last.T)
    out_ref[0:block] = dot(turned, rl)
    out_ref[block : 2 * block] = dot(turned, right3(part))
    out_ref[2 * block : 2 * block + block // 2 + 8] = pack(dot(turned, right3(c_last)))
    more_ref[...] = jnp.zeros_like(c_last)


def load(pairs, sems):
    copies = [pltpu.make_async_copy(source, target, sems.at[k]) for k, (source, target) in enumerate(pairs)]
    for copy in copies:
        copy.start()
    for copy in copies:
        copy.wait()


def cut(axis, c_ref, last):
    @pl.when(lax.axis_index(axis) == lax.axis_size(axis) - 1)
    def _():
        c_ref[last] = jnp.zeros_like(c_ref[last])


def edge(axis, s_hbm, d_hbm, c_hbm, odd_ref, s_ref, d_ref, c_ref, sems):
    nblocks, block, _ = d_hbm.shape
    last = nblocks - 1
    parity = lax.rem(lax.axis_index(axis), 2)
    swap_ref, more_ref = odd_ref.at[: odd_ref.shape[0] - block], odd_ref.at[odd_ref.shape[0] - block :]

    def bring(s_range, d_range, c_range):
        ranges = ((s_hbm, s_ref, s_range), (d_hbm, d_ref, d_range), (c_hbm, c_ref, c_range))
        load([(x.at[a:b], y.at[a:b]) for x, y, (a, b) in ranges], sems)

    @pl.when(parity == 0)
    def _():
        bring((0, 3), (0, 2), (0, 2))
        leftward(s_ref[0], s_ref[1], s_ref[2], symmetric(d_ref[0]), symmetric(d_ref[1]), c_ref[0], c_ref[1], swap_ref, more_ref)

    @pl.when(parity != 0)
    def _():
        bring((last - 1, nblocks), (last, nblocks), (last - 1, nblocks))
        cut(axis, c_ref, last)
        rightward(s_ref[last - 1], s_ref[last], symmetric(d_ref[last]), c_ref[last - 1], c_ref[last], swap_ref, more_ref)


def inner(axis, s_hbm, d_hbm, c_hbm, s_ref, even_ref, sym_ref, cl_ref, ct_ref, first_ref, pre_ref, pass_ref, d_ref, c_ref, sems):
    nblocks, block, _ = d_hbm.shape
    last = nblocks - 1
    parity = lax.rem(lax.axis_index(axis), 2)
    swap_ref, more_ref = even_ref.at[: even_ref.shape[0] - block], even_ref.at[even_ref.shape[0] - block :]
    load(((s_hbm, s_ref), (d_hbm, d_ref), (c_hbm, c_ref)), sems)
    cut(axis, c_ref, last)

    @pl.when(parity != 0)
    def _():
        leftward(s_ref[0], s_ref[1], s_ref[2], symmetric(d_ref[0]), symmetric(d_ref[1]), c_ref[0], c_ref[1], swap_ref, more_ref)

    @pl.when(parity == 0)
    def _():
        rightward(s_ref[last - 1], s_ref[last], symmetric(d_ref[last]), c_ref[last - 1], c_ref[last], swap_ref, more_ref)

    s = [s_ref[b] for b in range(nblocks)]
    sr = [right3(x) for x in s]
    for b in range(nblocks):
        sym_ref[b] = left3(symmetric(d_ref[b]))
        cl_ref[b] = left3(c_ref[b])
        ct_ref[b] = left3(c_ref[b].T)
    first = []
    for b in range(nblocks):
        acc = dot(sym_ref[b], sr[b])
        if b < last:
            acc += dot(cl_ref[b], sr[b + 1])
        if b > 0:
            acc += dot(ct_ref[b - 1], sr[b - 1])
        first.append(acc / half_width)
        first_ref[b] = first[b]
    pass_ref[...] = dot(ct_ref[last], sr[last])
    fr = [right3(x) for x in first]
    for b in range(nblocks):
        acc = None
        terms = []
        if 0 < b < last:
            terms.append((sym_ref, b, b))
        if b + 1 < last:
            terms.append((cl_ref, b, b + 1))
        if b > 1:
            terms.append((ct_ref, b - 1, b - 1))
        for ref, which, operand in terms:
            term = dot(ref[which], fr[operand])
            acc = term if acc is None else acc + term
        pre_ref[b] = -s[b] if acc is None else scale * acc - s[b]


def project(axis, s_ref, sym_ref, cl_ref, ct_ref, first_ref, pre_ref, pass_ref, even_ref, odd_ref, filt_ref, keep_ref, send_ref):
    nblocks, block, unused = s_ref.shape
    last = nblocks - 1
    parity = lax.rem(lax.axis_index(axis), 2)
    rows = odd_ref.shape[0] - block
    cuts = ((0, block), (block, 2 * block), (2 * block, rows))
    right = [jnp.where(parity == 0, even_ref[a:b], odd_ref[a:b]) for a, b in cuts]
    left = [jnp.where(parity == 0, odd_ref[a:b], even_ref[a:b]) for a, b in cuts]
    other = jnp.where(parity == 0, even_ref[rows:], odd_ref[rows:])
    onward = pass_ref[...]
    tail = first_ref[last] + dot(cl_ref[last], right3(right[0])) / half_width
    head = first_ref[0] + left[0] / half_width
    ahead = right[1] + onward / half_width
    behind = left[1] + dot(left3(unpack(left[2])), right3(s_ref[0])) / half_width
    tail_r, head_r = right3(tail), right3(head)
    filtered = [pre_ref[b] for b in range(nblocks)]
    filtered[0] += scale * (dot(sym_ref[0], head_r) + behind)
    filtered[1] += scale * dot(ct_ref[0], head_r)
    filtered[last - 1] += scale * dot(cl_ref[last - 1], tail_r)
    filtered[last] += scale * dot(beside(sym_ref[last], cl_ref[last]), stack(tail_r, right3(ahead)))
    beyond = other + scale * (dot(left3(unpack(right[2])), right3(onward)) / half_width + dot(ct_ref[last], tail_r))
    filtered.append(beyond)
    fr = [right3(x) for x in filtered]
    images = []
    for b in range(nblocks):
        filt_ref[b] = filtered[b]
        image = dot(beside(sym_ref[b] * 0.5, cl_ref[b]), stack(fr[b], fr[b + 1])) + 0.5 * center * filtered[b]
        images.append(image)
    total, fine = None, None
    for b in range(nblocks):
        (high, mid, low), (ihigh, imid, unused) = three(filtered[b]), three(images[b])
        upper = jnp.concatenate([jnp.concatenate([high, mid, high], 0), jnp.concatenate([ihigh, imid, ihigh], 0)], 1)
        term = dot(jnp.concatenate([high, high, mid], 0), upper, (0, 0))
        extra = dot(jnp.concatenate([high, low, mid], 0), jnp.concatenate([low, high, mid], 0), (0, 0))
        total = term if total is None else total + term
        fine = extra if fine is None else fine + extra
    width = filtered[0].shape[1]
    correlation, half = total[:, :width] + fine, total[:, width:]
    mixed = half + half.T
    rows, cols = iotas((width, width))
    packed = jnp.where(rows >= cols, correlation, mixed)
    diagonal = jnp.sum(jnp.where(rows == cols, mixed, 0.0), axis=0, keepdims=True)
    mid = width // 2

    def put(top_ref, low_ref):
        top_ref[0:mid, :] = packed[:mid]
        top_ref[mid : mid + 8, :] = jnp.broadcast_to(diagonal, (8, width))
        low_ref[0:mid, :] = packed[mid:]
        low_ref[mid : mid + 8, :] = jnp.broadcast_to(diagonal, (8, width))

    @pl.when(parity == 0)
    def _():
        put(keep_ref, send_ref)

    @pl.when(parity != 0)
    def _():
        put(send_ref, keep_ref)


def factor(full, inv_ref, group=8):
    width = full.shape[1]
    tiles = width // 8
    sub, lane = iotas((8, width))
    nought = jnp.where(lane < 0, 1.0, 0.0)

    def along(x, column):
        return jnp.broadcast_to(x[:, column : column + 1], (8, width))

    def down(x, row):
        return jnp.broadcast_to(x[row : row + 1, :], (8, width))

    work = [full[8 * t : 8 * t + 8, :] for t in range(tiles)]
    col, done = [], []
    for p in range(tiles):
        at = 8 * p
        start = p - p % group
        end = min(tiles, start + group)
        inside = (lane >= at) & (lane < at + 8)
        if p == start:
            done = []
            col = [along(work[p], at + j) for j in range(8)]
            col[0] = col[0] + nought
        raw = {(t, j): along(work[t], at + j) for j in range(8) for t in range(p + 1, end)}
        diagonal, recip, m = [], [], {}
        for j in range(8):
            diagonal.append(down(col[j], j))
            recip.append(1.0 / diagonal[j])
            ratio = col[j] * recip[j]
            for k in range(j + 1, 8):
                m[k, j] = down(ratio, k) if k > j + 2 else down(col[j], k) * recip[j]
                col[k] = col[k] - col[j] * m[k, j]
        coming = []
        if p + 1 < end:
            w = [raw[p + 1, j] for j in range(8)]
            w[0] = w[0] + nought
            coming = [along(work[p + 1], at + 8 + k) for k in range(8)]
            for j in range(8):
                for k in range(j + 1, 8):
                    w[k] = w[k] - w[j] * m[k, j]
                ratio = w[j] * recip[j]
                for k in range(8):
                    coming[k] = coming[k] - w[j] * down(ratio, k)
        cleared = jnp.where(inside, jnp.where(lane == sub + at, 1.0, 0.0), work[p])
        pivot = []
        for j in range(8):
            r = down(cleared, j)
            for k in range(j):
                r = r - m[j, k] * pivot[k]
            pivot.append(r)
        out = jnp.zeros((8, width), jnp.float32)
        for j in range(8):
            out = jnp.where(sub == j, pivot[j] * lax.rsqrt(diagonal[j]), out)
        inv_ref[at : at + 8, :] = jnp.where(lane <= sub + at, out, 0.0)
        done.append(jnp.where((lane > sub + at) & (lane < 8 * end), 0.0, out))
        solved = [None] * 8
        for k in reversed(range(8)):
            q = pivot[k] * recip[k]
            for j in reversed(range(k + 1, 8)):
                q = q - m[j, k] * solved[j]
            solved[k] = q
        for t in range(p + 1, end):
            acc = jnp.where(inside, 0.0, work[t])
            for j in reversed(range(8)):
                acc = acc - raw[t, j] * solved[j]
            work[t] = acc
        col = coming
        if p + 1 == end < tiles:
            rows = jnp.concatenate(done, 0)
            update = dot(left6(rows, 0), right6(rows, 0), (0, 0))
            for t in range(end, tiles):
                kept = jnp.where((lane >= 8 * start) & (lane < 8 * end), 0.0, work[t])
                work[t] = kept - update[8 * t : 8 * t + 8]


def finish(axis, total_nodes, mine_ref, other_ref, filt_ref, orth_hbm, proj_hbm, inv_ref, orth_ref, proj_ref, sems):
    nblocks, _, width = filt_ref.shape
    mid = width // 2
    swapped = lax.rem(lax.axis_index(axis), 2) != 0
    mine, other = mine_ref[...], other_ref[...]
    top = jnp.where(swapped, other, mine)
    low = jnp.where(swapped, mine, other)
    packed = jnp.concatenate([top[:mid], low[:mid]], 0)
    rows, cols = iotas((width, width))
    turned = packed.T
    full = jnp.where(rows >= cols, packed, turned)
    mixed = jnp.where(rows < cols, packed, jnp.where(rows > cols, turned, top[mid : mid + 1, :]))
    factor(full, inv_ref)
    inv = inv_ref[...]
    inv_r = right6(inv, 1)
    half = dot(left6(inv), right6(mixed))
    grown = right6(inv * math.sqrt(total_nodes), 1)
    copies = []

    def send(source, target):
        copies.append(pltpu.make_async_copy(source, target, sems.at[len(copies)]))
        copies[-1].start()

    for b in range(nblocks):
        orth_ref[b] = dot(left6(filt_ref[b]), grown, (1, 1))
        send(orth_ref.at[b], orth_hbm.at[b])
        if b == 0:
            proj_ref[...] = dot(left6(half), inv_r, (1, 1))
            send(proj_ref, proj_hbm)
    for copy in copies:
        copy.wait()


def shape(*dims, kind=jnp.float32):
    return jax.ShapeDtypeStruct(dims, kind)


def add_up(values, axis, stride=1):
    count = lax.axis_size(axis)
    index = lax.axis_index(axis)
    while stride < count:
        left = count // stride
        radix = 4 if left % 4 == 0 else next(r for r in range(2, left + 1) if left % r == 0)

        def route(partner):
            digits = [(i // stride) % radix for i in range(count)]
            return [(i, i + (partner(k) - k) * stride) for i, k in enumerate(digits)]

        if radix in (2, 4):
            parts = [values]
            for flip in range(1, radix):
                parts.append(lax.ppermute(values, axis, route((lambda k: (k - flip) % 4) if radix == 4 and stride > 2 else (lambda k: k ^ flip))))
            if radix == 4:
                parts = [parts[0], parts[2], parts[1], parts[3]]
            while len(parts) > 1:
                parts = [a + b for a, b in zip(parts[::2], parts[1::2])]
            values = parts[0]
        else:
            place = (index // stride) % radix
            parts = [values]
            for hop in range(1, radix):
                parts.append(lax.ppermute(values, axis, route(lambda k: (k - hop) % radix)))
            stacked = jnp.stack(parts)
            total = None
            for digit in range(radix):
                term = lax.dynamic_index_in_dim(stacked, (digit - place) % radix, 0, keepdims=False)
                total = term if total is None else total + term
            values = total
        stride *= radix
    return values


def swap(values, axis, start):
    count = lax.axis_size(axis)
    route = []
    for i in range(start, count - 1 + (start if count % 2 == 0 else 0), 2):
        other = (i + 1) % count
        route += [(i, other), (other, i)]
    return lax.ppermute(values, axis, route)


def body(states, diag_blocks, couplings):
    axis = "dom"
    nodes_dev, width = states.shape
    nblocks, block, _ = diag_blocks.shape
    devices = lax.axis_size(axis)
    field = states.reshape(nblocks, block, width)
    params = pltpu.CompilerParams(vmem_limit_bytes=40 << 20)
    cross = shape(3 * block + block // 2 + 8, width)
    tall = shape(nblocks, block, width)
    square = shape(nblocks, block, block)
    wide = shape(nblocks, block, 3 * block, kind=jnp.bfloat16)

    def call(kernel, ins, outs, scratch=()):
        return pl.pallas_call(
            kernel,
            out_shape=tuple(s for s, spec in outs),
            in_specs=ins,
            out_specs=tuple(spec for s, spec in outs),
            scratch_shapes=scratch,
            compiler_params=params,
        )

    inputs = tuple(pltpu.with_memory_space_constraint(x, pltpu.HBM) for x in (field, diag_blocks, couplings))
    squares = [pltpu.VMEM(square.shape, jnp.float32)] * 2 + [pltpu.SemaphoreType.DMA((3,))]
    (odd,) = call(
        lambda *refs: edge(axis, *refs), [far] * 3, [(cross, here)], [pltpu.VMEM(tall.shape, jnp.float32)] + squares
    )(*inputs)
    odd = swap(odd, axis, 1)
    s, even, sym, cl, ct, first, pre, onward = call(
        lambda *refs: inner(axis, *refs),
        [far] * 3,
        [(tall, here), (cross, here), (wide, here), (wide, here), (wide, here), (tall, here), (tall, here), (shape(block, width), here)],
        squares,
    )(*inputs)
    even = swap(even, axis, 0)
    piece = shape(width // 2 + 8, width)
    filtered, keep, send = call(
        lambda *refs: project(axis, *refs), [here] * 9, [(tall, here), (piece, here), (piece, here)]
    )(s, sym, cl, ct, first, pre, onward, even, odd)
    mine = add_up(keep + swap(send, axis, 0), axis, 2)
    other = swap(mine, axis, 0)
    orthonormal, projected = call(
        lambda *refs: finish(axis, nodes_dev * devices, *refs),
        [here] * 3,
        [(tall, far), (shape(width, width), far)],
        [
            pltpu.VMEM((width, width), jnp.float32),
            pltpu.VMEM((nblocks, block, width), jnp.float32),
            pltpu.VMEM((width, width), jnp.float32),
            pltpu.SemaphoreType.DMA((nblocks + 1,)),
        ],
    )(mine, other, filtered)
    return orthonormal.reshape(nodes_dev, width), projected


def solution(mesh):
    in_specs = (P("dom", None), P("dom", None, None), P("dom", None, None))
    out_specs = (P("dom", None), P())

    return jax.shard_map(body, mesh=mesh, in_specs=in_specs, out_specs=out_specs, check_vma=False)
```
